128 devices in a mesh: rep: 8 (over z, core), pipe: 8 (over y_lo, x), tp: 2 (over y_hi).
Axes of the slice: x: 4, y: 4 (y_hi: 2, y_lo: 2; y = y_hi * 2 + y_lo), z: 4, core: 2. Of those that a mesh axis runs over, the one named last changes fastest.
Arguments:
- fwd_in: bfloat16 [8, 8, 256, 3072], P('rep', 'pipe', None, 'tp'), may hold values from -6 to 6
- bwd_in: bfloat16 [8, 8, 256, 3072], P('rep', 'pipe', None, 'tp'), may hold values from -6 to 6
- bwd_grad: bfloat16 [8, 8, 256, 3072], P('rep', 'pipe', None, 'tp'), may hold values from -18 to 18
- seg_fwd: int32 [8, 8, 256], P('rep', 'pipe'), may hold values from 0 to 3, never falling along the last dimension, each value on 1 to 128 neighbouring positions
- seg_bwd: int32 [8, 8, 256], P('rep', 'pipe'), may hold values from 0 to 3, never falling along the last dimension, each value on 1 to 128 neighbouring positions
- w_query: bfloat16 [8, 8, 3072, 3072], P('rep', 'pipe', None, 'tp'), may hold values from -6 to 6
- w_key: bfloat16 [8, 8, 3072, 128], P('rep', 'pipe'), may hold values from -60 to 60
- gain: bfloat16 [8, 8, 3072], P('rep', 'pipe', 'tp'), may hold values from 0.5 to 1.5
- gossip_exp: int32 [8], P('pipe'), may hold values from 0 to 2
Outputs:
- next_input: bfloat16 [8, 8, 256, 3072], P('rep', 'pipe', None, 'tp')
- prev_grad: bfloat16 [8, 8, 256, 3072], P('rep', 'pipe', None, 'tp')
- w_query_out: bfloat16 [8, 8, 3072, 3072], P('rep', 'pipe', None, 'tp')
- w_key_out: bfloat16 [8, 8, 3072, 128], P('rep', 'pipe')
- gain_out: bfloat16 [8, 8, 3072], P('rep', 'pipe', 'tp')
The draws below stay inside these ranges and needn't reach their ends.
Inputs may be any that keep to these rules, and one draw needn't show every extreme that they name: The partner of replica r at section p is r XOR 2^k with k = gossip_exp[p]. `seg_fwd`: along each section's rows the caption ids never fall; each caption has 1 to 128 tokens. `seg_bwd`: along each section's rows the caption ids never fall; each caption has 1 to 128 tokens.
All inputs are finite; a program needn't handle non-finite values.
Results may differ from the reference program's by a relative error of at most 0.015.
The reference program's roundings to bfloat16 on the way count: a program that leaves them out, or rounds other values in their place, can miss the bound.
Values may be sent and summed in bfloat16 or wider, within the bound.
A program may use at most 192 MiB of HBM per device.

```python
import math
import jax
import jax.numpy as jnp
import numpy as np
from jax import lax

HEAD = 128
HEADS = 24
D = 3072
ROWS = 256
CAPTIONS = 4
CAP_MOST = 128
REPLICAS = 8
SECTIONS = 8
N_REP = 8


def draw_w_query(key, part):
    leading = jax.random.normal(jax.random.fold_in(key, 11), (REPLICAS, SECTIONS, D, HEAD), jnp.float32)
    others = jax.random.normal(jax.random.fold_in(key, 12), (REPLICAS, SECTIONS, D, D - HEAD), jnp.float32)
    return jnp.clip(jnp.concatenate([leading, others], axis=3), -6.0, 6.0).astype(jnp.bfloat16)


def draw_w_key(key, part):
    base = jnp.clip(jax.random.normal(jax.random.fold_in(key, 13), (REPLICAS, SECTIONS, D, HEAD), jnp.float32), -6.0, 6.0)
    return base.astype(jnp.bfloat16)


def draw_bwd_grad(key, part):
    shape = (REPLICAS, SECTIONS, ROWS, D)
    ramp = jnp.arange(SECTIONS, dtype=jnp.float32) / max(SECTIONS - 1, 1)
    noise = jnp.clip(jax.random.normal(jax.random.fold_in(key, 22), shape, jnp.float32), -6.0, 6.0)
    factor = 1.0 + 2.0 * ramp
    return (noise * factor[None, :, None, None]).astype(jnp.bfloat16)


def with_ends(array, rng, least, high):
    longest = array.shape.index(max(array.shape))
    spots = []
    for shift in (0, 1):
        where = [jax.random.randint(jax.random.fold_in(rng, axis), (), 0, length) for axis, length in enumerate(array.shape)]
        where[longest] = (where[longest] + shift) % array.shape[longest]
        spots.append(tuple(where))
    return array.at[spots[0]].set(least).at[spots[1]].set(high)


def levels(key, shape, shards, least, top_value):
    loudness = 1.0
    for axis_at, blocks in shards:
        draws = jax.random.uniform(jax.random.fold_in(jax.random.fold_in(key, 6), axis_at), (blocks,), jnp.float32, least / len(shards), top_value / len(shards))
        loudness = loudness * jnp.repeat(jnp.exp(draws), shape[axis_at] // blocks).reshape((-1,) + (1,) * (len(shape) - 1 - axis_at))
    return loudness


def profile(amount, total, limit, lean):
    loads = [(1 << 20) // math.isqrt(grade ** lean) + 1 for grade in range(2, amount + 1)]
    rest, counts = total - limit - (amount - 1), [1] * (amount - 1)
    while rest > 0:
        movable = [i for i in range(amount - 1) if counts[i] < limit]
        pool, budget = sum([loads[i] for i in movable]), rest
        for i in movable:
            addition = min(limit - counts[i], max(1, budget * loads[i] // pool), rest)
            counts[i] = counts[i] + addition
            rest = rest - addition
    return np.array([limit] + counts)


def ragged(stream_key, amount, total, most, skew):
    if amount == 2:
        one = jax.random.randint(stream_key, (), max(1, total - most), min(most, total - 1) + 1)
        return jnp.stack([one, total - one])
    tallies = jnp.asarray(profile(amount, total, most, skew), jnp.int32)
    twos = (amount - 1) // 2
    giver, receiver = tallies[1:1 + 2 * twos:2], tallies[2:2 + 2 * twos:2]
    slack = jnp.minimum(giver - 1, most - receiver)
    moved = jax.random.randint(jax.random.fold_in(stream_key, 1), (twos,), 0, 1 << 20) % (slack + 1)
    tallies = tallies.at[1:1 + 2 * twos:2].set(giver - moved).at[2:2 + 2 * twos:2].set(receiver + moved)
    return tallies[jax.random.permutation(jax.random.fold_in(stream_key, 2), amount)]


def scatter_about(key, shape, width, reach, pieces=(), kind=jnp.bfloat16):
    entries = width * jax.random.normal(key, shape, jnp.float32)
    if pieces:
        entries = entries * levels(key, shape, pieces, -0.22, 0.18)
    return jnp.clip(entries, -reach, reach).astype(kind)


def setup_inputs(seed: int = 0) -> dict:
    seeds = jax.random.split(jax.random.key(seed), 10)
    return {
        "fwd_in": scatter_about(seeds[0], (REPLICAS, SECTIONS, ROWS, D), 1.0, 6.0, ((0, 8), (1, 8), (3, 2))),
        "bwd_in": scatter_about(seeds[1], (REPLICAS, SECTIONS, ROWS, D), 1.0, 6.0, ((0, 8), (1, 8), (3, 2))),
        "bwd_grad": draw_bwd_grad(jax.random.fold_in(seeds[9], 71), 0),
        "seg_fwd": jax.vmap(lambda own: jnp.searchsorted(jnp.cumsum(ragged(own, CAPTIONS, ROWS, CAP_MOST, 1)), jnp.arange(ROWS), side="right"))(jax.random.split(seeds[3], REPLICAS * SECTIONS)).reshape((REPLICAS, SECTIONS, ROWS)).astype(jnp.int32),
        "seg_bwd": jax.vmap(lambda own: jnp.searchsorted(jnp.cumsum(ragged(own, CAPTIONS, ROWS, CAP_MOST, 1)), jnp.arange(ROWS), side="right"))(jax.random.split(seeds[4], REPLICAS * SECTIONS)).reshape((REPLICAS, SECTIONS, ROWS)).astype(jnp.int32),
        "w_query": draw_w_query(jax.random.fold_in(seeds[9], 71), 0),
        "w_key": draw_w_key(jax.random.fold_in(seeds[9], 71), 0),
        "gain": jnp.clip(1.0 + 0.1 * jax.random.normal(seeds[7], (REPLICAS, SECTIONS, D), jnp.float32), 0.5, 1.5).astype(jnp.bfloat16),
        "gossip_exp": with_ends(jax.random.randint(seeds[8], (SECTIONS,), 0, N_REP // 4 + 1), jax.random.fold_in(seeds[8], 1), 0, (N_REP // 4 + 1) - 1).astype(jnp.int32),
    }


LN_EPS = 1e-05
STEP_EPS = 1e-06
LEARN_RATE = 0.2
MASK_FILL = -1e+30

def normalize(rows, gain_row):
    values = rows.astype(jnp.float32)
    centred = values - lax.optimization_barrier(jnp.mean(values, axis=-1, keepdims=True))
    inv_std = lax.rsqrt(lax.optimization_barrier(jnp.mean(centred * centred, axis=-1, keepdims=True)) + LN_EPS)
    scaled = centred * inv_std
    normed = (scaled * gain_row.astype(jnp.float32)).astype(jnp.bfloat16)
    return (values, scaled, inv_std, normed)

def attend(normed, caption, query_weight, key_weight):
    in_scale = D ** (-0.5)
    count = normed.shape[0]
    queries = (jnp.dot(normed, query_weight, preferred_element_type=jnp.float32) * in_scale).astype(jnp.bfloat16)
    keys = (jnp.dot(normed, key_weight, preferred_element_type=jnp.float32) * in_scale).astype(jnp.bfloat16)
    query_heads = queries.reshape(count, HEADS, HEAD).astype(jnp.float32)
    value_heads = normed.reshape(count, HEADS, HEAD).astype(jnp.float32)
    key_rows = keys.astype(jnp.float32)
    scores = jnp.einsum('rhd,sd->hrs', query_heads, key_rows) * HEAD ** (-0.5)
    same = caption[:, None] == caption[None, :]
    scores = jnp.where(same[None], scores, MASK_FILL)
    peak = lax.optimization_barrier(jnp.max(scores, axis=-1, keepdims=True))
    expo = jnp.exp(scores - peak)
    probs = (expo / lax.optimization_barrier(jnp.sum(expo, axis=-1, keepdims=True))).astype(jnp.bfloat16)
    mixed = jnp.einsum('hrs,shd->rhd', probs.astype(jnp.float32), value_heads).reshape(count, D)
    return (query_heads, key_rows, value_heads, probs, mixed)

def section(items):
    fwd_rows, bwd_rows, grad_rows, seg_fwd, seg_bwd, query_weight, key_weight, gain_row = items
    in_scale = D ** (-0.5)
    count = fwd_rows.shape[0]
    values, scaled, inv_std, normed = normalize(fwd_rows, gain_row)
    mixed = attend(normed, seg_fwd, query_weight, key_weight)[4]
    section_out = (values + mixed).astype(jnp.bfloat16)
    values_b, scaled_b, inv_b, normed_b = normalize(bwd_rows, gain_row)
    query_heads, key_rows, value_heads, probs, unused = attend(normed_b, seg_bwd, query_weight, key_weight)
    grad_heads = grad_rows.astype(jnp.float32).reshape(count, HEADS, HEAD)
    prob_f = probs.astype(jnp.float32)
    value_grad = jnp.einsum('hrs,rhd->shd', prob_f, grad_heads).reshape(count, D)
    prob_grad = jnp.einsum('rhd,shd->hrs', grad_heads, value_heads)
    score_grad = (prob_f * (prob_grad - lax.optimization_barrier(jnp.sum(prob_grad * prob_f, axis=-1, keepdims=True))) * HEAD ** (-0.5)).astype(jnp.bfloat16)
    score_f = score_grad.astype(jnp.float32)
    query_grad = jnp.einsum('hrs,sd->rhd', score_f, key_rows).reshape(count, D).astype(jnp.bfloat16)
    key_grad = jnp.einsum('hrs,rhd->sd', score_f, query_heads).astype(jnp.bfloat16)
    normed_grad = (jnp.dot(query_grad, query_weight.T, preferred_element_type=jnp.float32) + jnp.dot(key_grad, key_weight.T, preferred_element_type=jnp.float32)) * in_scale + value_grad
    scaled_grad = normed_grad * gain_row.astype(jnp.float32)
    input_grad = inv_b * (scaled_grad - lax.optimization_barrier(jnp.mean(scaled_grad, axis=-1, keepdims=True)) - scaled_b * lax.optimization_barrier(jnp.mean(scaled_grad * scaled_b, axis=-1, keepdims=True)))
    back_rows = (grad_rows.astype(jnp.float32) + input_grad).astype(jnp.bfloat16)
    grad_query = jnp.dot(normed_b.T, query_grad, preferred_element_type=jnp.float32) * in_scale
    grad_key = jnp.dot(normed_b.T, key_grad, preferred_element_type=jnp.float32) * in_scale
    grad_gain = lax.optimization_barrier(jnp.sum(normed_grad * scaled_b, axis=0))
    squares = jnp.sum(grad_query * grad_query) + jnp.sum(grad_key * grad_key) + jnp.sum(grad_gain * grad_gain)
    return (section_out, back_rows, grad_query, grad_key, grad_gain, squares)

def replica_step(items):
    outs = lax.map(section, items)
    section_out, back_rows, grad_query, grad_key, grad_gain, squares = outs
    total = SECTIONS * (D * D + D * HEAD + D)
    inverse = lax.rsqrt(jnp.sum(squares) / total + STEP_EPS)
    step_query = (LEARN_RATE * grad_query * inverse).astype(jnp.bfloat16)
    step_key = (LEARN_RATE * grad_key * inverse).astype(jnp.bfloat16)
    step_gain = (LEARN_RATE * grad_gain * inverse).astype(jnp.bfloat16)
    return (section_out, back_rows, step_query, step_key, step_gain)

def updated(weight, step):
    return (weight.astype(jnp.float32) - step.astype(jnp.float32)).astype(jnp.bfloat16)

def average(own, partner, own_step, partner_step):
    mine = updated(own, own_step).astype(jnp.float32)
    theirs = updated(partner, partner_step).astype(jnp.float32)
    return ((mine + theirs) * 0.5).astype(jnp.bfloat16)

def reference(fwd_in, bwd_in, bwd_grad, seg_fwd, seg_bwd, w_query, w_key, gain, gossip_exp):
    section_out, back_rows, step_query, step_key, step_gain = lax.map(replica_step, (fwd_in, bwd_in, bwd_grad, seg_fwd, seg_bwd, w_query, w_key, gain))
    next_input = jnp.roll(section_out, 1, axis=1)
    prev_grad = jnp.roll(back_rows, -1, axis=1)
    distance = jnp.left_shift(jnp.int32(1), gossip_exp.astype(jnp.int32))
    section_ids = jnp.arange(SECTIONS, dtype=jnp.int32)

    def combine(index):
        others = jnp.bitwise_xor(index, distance).astype(jnp.int32)
        return (average(w_query[index], w_query[others, section_ids], step_query[index], step_query[others, section_ids]), average(w_key[index], w_key[others, section_ids], step_key[index], step_key[others, section_ids]), average(gain[index], gain[others, section_ids], step_gain[index], step_gain[others, section_ids]))
    w_query_out, w_key_out, gain_out = lax.map(combine, jnp.arange(REPLICAS, dtype=jnp.int32))
    return (next_input, prev_grad, w_query_out, w_key_out, gain_out)
```

```python
from functools import partial

import jax
import jax.numpy as jnp
from jax import lax
from jax.sharding import PartitionSpec as P

HEAD = 128


LN_EPS = 1e-05
STEP_EPS = 1e-06
LEARN_RATE = 0.2
MASK_FILL = -1e30
CHUNKS = 2


def from_behind(shard, axis, by):
    length = lax.axis_size(axis)
    return lax.ppermute(shard, axis, [(i, (i + by) % length) for i in range(length)])


def flipped(block, axis, bit):
    return lax.ppermute(block, axis, [(i, i ^ 1 << bit) for i in range(lax.axis_size(axis))])


def in_order(own, other, low, axis):
    return jnp.where(
        low, jnp.concatenate([own, other], axis), jnp.concatenate([other, own], axis)
    )


def of_everyone(shard, axis):
    copies = jnp.broadcast_to(shard, (lax.axis_size(axis), *shard.shape))
    return jnp.sum(lax.all_to_all(copies, axis, split_axis=0, concat_axis=0, tiled=True), axis=0)


class Gossip:
    def __init__(self, exponent):
        self.exponent = exponent
        self.odd = (lax.axis_index("rep") // 2) % 2
        self.one = exponent == 1

    def first(self, up, down):
        return from_behind(up, "rep", 2), from_behind(down, "rep", -2), up, down

    def second(self, state):
        above, below, up, down = state
        return (
            from_behind(jnp.where(self.one, down, above), "rep", 2),
            from_behind(jnp.where(self.one, up, below), "rep", -2),
        )

    def case(self):
        return jnp.where(self.exponent == 2, 3, jnp.where(self.one, 1 + self.odd, 0))

    def choices(self, near, state, later):
        above, below = state[:2]
        from_up, from_down = later
        return (near, (from_down, below), (above, from_up), (from_up, from_down))

    def pick(self, near, state, later):
        sets = self.choices(near, state, later)
        case = self.case()
        return [
            jnp.where(case == 0, a, jnp.where(case == 1, b, jnp.where(case == 2, c, d)))
            for a, b, c, d in zip(*sets)
        ]

    def small(self, block):
        half = block.shape[0] // 2
        up, down = block[:half], block[half:]
        state = self.first(up, down)
        later = self.second(state)
        near = flipped(block, "rep", 0)
        return jnp.concatenate(self.pick((near[:half], near[half:]), state, later), axis=0)

    def tiny(self, block):
        results = [flipped(block, "rep", bit) for bit in range(3)]
        return jnp.where(
            self.exponent == 0, results[0], jnp.where(self.one, results[1], results[2])
        )


def normalize(rows, gain_full):
    values = rows.astype(jnp.float32)
    centred = values - jnp.mean(values, axis=-1, keepdims=True)
    inv_std = lax.rsqrt(jnp.mean(centred * centred, axis=-1, keepdims=True) + LN_EPS)
    scaled = centred * inv_std
    normed = (scaled * gain_full.astype(jnp.float32)).astype(jnp.bfloat16)
    return (values, scaled, inv_std, normed)


def attend(normed, value_rows, caption, query_weight, key_weight):
    in_scale = normed.shape[1] ** (-0.5)
    count = normed.shape[0]
    heads = query_weight.shape[1] // HEAD
    queries = (jnp.dot(normed, query_weight, preferred_element_type=jnp.float32) * in_scale).astype(
        jnp.bfloat16
    )
    keys = (jnp.dot(normed, key_weight, preferred_element_type=jnp.float32) * in_scale).astype(
        jnp.bfloat16
    )
    query_heads = queries.reshape(count, heads, HEAD)
    value_heads = value_rows.reshape(count, heads, HEAD)
    scores = jnp.einsum(
        "rhd,sd->hrs", query_heads, keys, preferred_element_type=jnp.float32
    ) * HEAD ** (-0.5)
    same = caption[:, None] == caption[None, :]
    scores = jnp.where(same[None], scores, MASK_FILL)
    peak = jnp.max(scores, axis=-1, keepdims=True)
    expo = jnp.exp(scores - peak)
    probs = (expo / jnp.sum(expo, axis=-1, keepdims=True)).astype(jnp.bfloat16)
    return (query_heads, keys, value_heads, probs)


def updated(weight, step):
    return (weight.astype(jnp.float32) - step.astype(jnp.float32)).astype(jnp.bfloat16)


def halves(mine, theirs):
    return ((mine.astype(jnp.float32) + theirs.astype(jnp.float32)) * 0.5).astype(jnp.bfloat16)


def shards(fwd_in, bwd_in, bwd_grad, seg_fwd, seg_bwd, w_query, w_key, gain, gossip_exp):
    query_weight = w_query[0, 0]
    key_weight = w_key[0, 0]
    gain_local = gain[0, 0]
    fwd_rows = fwd_in[0, 0]
    bwd_rows = bwd_in[0, 0]
    grad_rows = bwd_grad[0, 0]
    count, local_width = fwd_rows.shape
    tp_count = lax.axis_size("tp")
    pipe_count = lax.axis_size("pipe")
    tp_index = lax.axis_index("tp")
    low = tp_index == 0
    offset = tp_index * local_width
    gossip = Gossip(gossip_exp[0])

    bwd_full = in_order(bwd_rows, flipped(bwd_rows, "tp", 0), low, 1)
    gain_full = in_order(gain_local, flipped(gain_local, "tp", 0), low, 0)
    width = bwd_full.shape[1]
    in_scale = width ** (-0.5)

    step_rows = width // (2 * CHUNKS)
    parts = [query_weight[i * step_rows : (i + 1) * step_rows] for i in range(2 * CHUNKS)]
    sent = [gossip.first(parts[i], parts[CHUNKS + i]) for i in range(CHUNKS)]
    query_near = flipped(query_weight, "rep", 0)

    values_b, scaled_b, inv_b, normed_b = normalize(bwd_full, gain_full)
    own_values_b = lax.dynamic_slice_in_dim(normed_b, offset, local_width, 1)
    normed_half = gossip.small(own_values_b)
    normed_partner = in_order(normed_half, flipped(normed_half, "tp", 0), low, 1)
    key_half = gossip.small(lax.dynamic_slice_in_dim(key_weight, offset, local_width, 0))
    key_partner = in_order(key_half, flipped(key_half, "tp", 0), low, 0)

    query_heads, keys, value_heads, probs = attend(
        normed_b, own_values_b, seg_bwd[0, 0], query_weight, key_weight
    )
    heads = local_width // HEAD
    grad_heads = grad_rows.reshape(count, heads, HEAD)
    prob_grad = jnp.einsum(
        "rhd,shd->hrs", grad_heads, value_heads, preferred_element_type=jnp.float32
    )
    prob_f = probs.astype(jnp.float32)
    score_grad = (
        prob_f * (prob_grad - jnp.sum(prob_grad * prob_f, axis=-1, keepdims=True)) * HEAD ** (-0.5)
    ).astype(jnp.bfloat16)
    query_grad = (
        jnp.einsum("hrs,sd->rhd", score_grad, keys, preferred_element_type=jnp.float32)
        .reshape(count, local_width)
        .astype(jnp.bfloat16)
    )
    query_grad_partner = gossip.small(query_grad)
    key_part = jnp.einsum(
        "hrs,rhd->sd", score_grad, query_heads, preferred_element_type=jnp.float32
    ).astype(jnp.bfloat16)
    key_grad = (
        key_part.astype(jnp.float32) + flipped(key_part, "tp", 0).astype(jnp.float32)
    ).astype(jnp.bfloat16)
    key_grad_partner = gossip.small(key_grad)
    value_grad = jnp.einsum(
        "hrs,rhd->shd", probs, grad_heads, preferred_element_type=jnp.float32
    ).reshape(count, local_width)

    contract_last = (((1,), (1,)), ((), ()))
    partial_grad = (
        lax.dot_general(query_grad, query_weight, contract_last, preferred_element_type=jnp.float32)
        * in_scale
    )
    own_part = (lax.dynamic_slice_in_dim(partial_grad, offset, local_width, 1) + value_grad).astype(
        jnp.bfloat16
    )
    other_part = lax.dynamic_slice_in_dim(
        partial_grad, local_width - offset, local_width, 1
    ).astype(jnp.bfloat16)
    from_other = flipped(other_part, "tp", 0)
    key_rows = lax.dynamic_slice_in_dim(key_weight, offset, local_width, 0)
    full_grad = (
        own_part.astype(jnp.float32)
        + from_other.astype(jnp.float32)
        + lax.dot_general(key_grad, key_rows, contract_last, preferred_element_type=jnp.float32)
        * in_scale
    )
    own_scaled = lax.dynamic_slice_in_dim(scaled_b, offset, local_width, 1)
    weighted = full_grad * gain_local.astype(jnp.float32)
    sums = jnp.stack([jnp.sum(weighted, axis=-1), jnp.sum(weighted * own_scaled, axis=-1)])
    means = (sums + flipped(sums, "tp", 0)) / width
    input_grad = inv_b * (weighted - means[0][:, None] - own_scaled * means[1][:, None])
    grad_gain = jnp.sum(full_grad * own_scaled, axis=0)
    back_rows = (grad_rows.astype(jnp.float32) + input_grad).astype(jnp.bfloat16)
    prev_rows = from_behind(back_rows, "pipe", -1)

    fwd_full = in_order(fwd_rows, flipped(fwd_rows, "tp", 0), low, 1)
    values, scaled, inv_std, normed = normalize(fwd_full, gain_full)
    own_values = lax.dynamic_slice_in_dim(normed, offset, local_width, 1)
    unused_q, unused_k, value_heads_f, probs_f = attend(
        normed, own_values, seg_fwd[0, 0], query_weight, key_weight
    )
    mixed = jnp.einsum(
        "hrs,shd->rhd", probs_f, value_heads_f, preferred_element_type=jnp.float32
    ).reshape(count, -1)
    section_out = (fwd_rows.astype(jnp.float32) + mixed).astype(jnp.bfloat16)
    next_rows = from_behind(section_out, "pipe", 1)

    contract_first = (((0,), (0,)), ((), ()))

    def weight_grad(rows, grad):
        return (
            lax.dot_general(rows, grad, contract_first, preferred_element_type=jnp.float32)
            * in_scale
        )

    grad_query = weight_grad(normed_b, query_grad)
    grad_key = weight_grad(normed_b, key_grad)
    local_squares = (
        jnp.sum(grad_query * grad_query)
        + jnp.sum(grad_gain * grad_gain)
        + jnp.sum(grad_key * grad_key) / tp_count
    )
    total_squares = of_everyone(local_squares, ("pipe", "tp"))
    total = pipe_count * (width * width + width * HEAD + width)
    inverse = lax.rsqrt(total_squares / total + STEP_EPS)

    def step_of(gradient, scale):
        return (LEARN_RATE * gradient * scale).astype(jnp.bfloat16)

    gain_new = updated(gain_local, step_of(grad_gain, inverse))
    both = gossip.tiny(
        jnp.concatenate(
            [gain_new.astype(jnp.float32), jnp.broadcast_to(inverse, (HEAD,))]
        )
    )
    gain_partner = both[:local_width].astype(jnp.bfloat16)
    inverse_partner = both[local_width]
    gain_out = halves(gain_new, gain_partner)

    key_out = halves(
        updated(key_weight, step_of(grad_key, inverse)),
        updated(
            key_partner,
            step_of(weight_grad(normed_partner, key_grad_partner), inverse_partner),
        ),
    )
    query_new = updated(query_weight, step_of(grad_query, inverse))
    query_step_partner = step_of(weight_grad(normed_partner, query_grad_partner), inverse_partner)

    later = [gossip.second(state) for state in sent]
    ups, downs = zip(*later)
    nears = [query_near[i * step_rows : (i + 1) * step_rows] for i in range(2 * CHUNKS)]
    candidates = [
        gossip.choices((nears[i], nears[CHUNKS + i]), sent[i], later[i]) for i in range(CHUNKS)
    ]

    def averaged(case, candidates, new, step):
        picked = [c[case] for c in candidates]
        weight = jnp.concatenate([p[0] for p in picked] + [p[1] for p in picked], axis=0)
        return halves(new, updated(weight, step))

    query_out = lax.switch(
        gossip.case(),
        [partial(averaged, case) for case in range(4)],
        candidates,
        query_new,
        query_step_partner,
    )
    return (
        next_rows[None, None],
        prev_rows[None, None],
        query_out[None, None],
        key_out[None, None],
        gain_out[None, None],
    )


def solution(mesh):
    return jax.shard_map(
        shards,
        mesh=mesh,
        in_specs=(
            P("rep", "pipe", None, "tp"),
            P("rep", "pipe", None, "tp"),
            P("rep", "pipe", None, "tp"),
            P("rep", "pipe", None),
            P("rep", "pipe", None),
            P("rep", "pipe", None, "tp"),
            P("rep", "pipe", None, None),
            P("rep", "pipe", "tp"),
            P("pipe"),
        ),
        out_specs=(
            P("rep", "pipe", None, "tp"),
            P("rep", "pipe", None, "tp"),
            P("rep", "pipe", None, "tp"),
            P("rep", "pipe", None, None),
            P("rep", "pipe", "tp"),
        ),
        check_vma=False,
    )
```

```python
import jax
import jax.numpy as jnp
from jax import lax
from jax.experimental import pallas as pl
from jax.experimental.pallas import tpu as pltpu
from jax.sharding import PartitionSpec as P


HEAD = 128


LN_EPS = 1e-05
STEP_EPS = 1e-06
LEARN_RATE = 0.2
MASK_FILL = -1e30
CHUNK_SHARES = (2, 3, 1)
BLOCK = 256


def from_behind(shard, axis, by):
    length = lax.axis_size(axis)
    return lax.ppermute(shard, axis, [(i, (i + by) % length) for i in range(length)])


def flipped(block, axis, bit):
    return lax.ppermute(block, axis, [(i, i ^ 1 << bit) for i in range(lax.axis_size(axis))])


def in_order(own, other, low, axis):
    return jnp.where(
        low, jnp.concatenate([own, other], axis), jnp.concatenate([other, own], axis)
    )


def of_everyone(shard, axis):
    copies = jnp.broadcast_to(shard, (lax.axis_size(axis), *shard.shape))
    return jnp.sum(lax.all_to_all(copies, axis, split_axis=0, concat_axis=0, tiled=True), axis=0)


def chunk_cuts(rows):
    whole, edges = sum(CHUNK_SHARES), [0]
    for share in CHUNK_SHARES:
        edges.append(edges[-1] + rows * share // whole)
    return list(zip(edges[:-1], edges[1:]))


def relay_kernel(case_ref, up, down, above_in, below_in, above, below, held, sem):
    def carry(source, target):
        for one, other in ((source, held), (held, target)):
            copy = pltpu.make_async_copy(one, other, sem)
            copy.start()
            copy.wait()

    @pl.when(case_ref[0] == 1)
    def _():
        carry(down, above)

    @pl.when(case_ref[0] == 2)
    def _():
        carry(up, below)


def relayed(case, up, down, above, below):
    anywhere = pl.BlockSpec(memory_space=pl.ANY)
    return pl.pallas_call(
        relay_kernel,
        in_specs=[pl.BlockSpec(memory_space=pltpu.SMEM)] + [anywhere] * 4,
        out_specs=[anywhere] * 2,
        out_shape=[jax.ShapeDtypeStruct(up.shape, up.dtype)] * 2,
        input_output_aliases={3: 0, 4: 1},
        scratch_shapes=[pltpu.VMEM(up.shape, up.dtype), pltpu.SemaphoreType.DMA],
        cost_estimate=pl.CostEstimate(flops=0, bytes_accessed=up.size, transcendentals=0),
        compiler_params=pltpu.CompilerParams(vmem_limit_bytes=8 << 20),
    )(case.reshape(1), up, down, above, below)


class Gossip:
    def __init__(self, exponent):
        self.exponent = exponent
        odd = (lax.axis_index("rep") // 2) % 2
        self.case = jnp.where(exponent == 2, 3, jnp.where(exponent == 1, 1 + odd, 0))

    def first(self, up, down):
        return up, down, from_behind(up, "rep", 2), from_behind(down, "rep", -2)

    def second(self, state):
        above, below = relayed(self.case, *state)
        return above, below, from_behind(above, "rep", 2), from_behind(below, "rep", -2)

    def small(self, block):
        half = block.shape[0] // 2
        up, down, block = lax.optimization_barrier((block[:half], block[half:], block))
        state = self.first(up, down)
        above, below, from_up, from_down = self.second(state)
        near = flipped(block, "rep", 0)
        case = self.case

        def pick(a, b, c, d):
            return jnp.where(case == 0, a, jnp.where(case == 1, b, jnp.where(case == 2, c, d)))

        return jnp.concatenate(
            [
                pick(near[:half], from_down, above, from_up),
                pick(near[half:], below, from_up, from_down),
            ],
            axis=0,
        )

    def tiny(self, block):
        results = [flipped(block, "rep", bit) for bit in range(3)]
        return jnp.where(
            self.exponent == 0, results[0], jnp.where(self.exponent == 1, results[1], results[2])
        )


def normalize(rows, gain_full):
    values = rows.astype(jnp.float32)
    centred = values - jnp.mean(values, axis=-1, keepdims=True)
    inv_std = lax.rsqrt(jnp.mean(centred * centred, axis=-1, keepdims=True) + LN_EPS)
    scaled = centred * inv_std
    normed = (scaled * gain_full.astype(jnp.float32)).astype(jnp.bfloat16)
    return (values, scaled, inv_std, normed)


def projected(normed, weight):
    in_scale = normed.shape[1] ** (-0.5)
    product = jnp.dot(normed, weight, preferred_element_type=jnp.float32)
    return (product * in_scale).astype(jnp.bfloat16)


def dot(a, b, over):
    return lax.dot_general(a, b, (over, ((), ())), preferred_element_type=jnp.float32)


ROWS_COLS, LAST_LAST, FIRST_FIRST = ((1,), (0,)), ((1,), (1,)), ((0,), (0,))


def head_probs(queries, keys, tall, wide):
    scores = dot(queries, keys, LAST_LAST) * HEAD ** (-0.5)
    scores = jnp.where(tall == wide, scores, MASK_FILL)
    peak = jnp.max(scores, axis=-1, keepdims=True)
    expo = jnp.exp(scores - peak)
    return (expo / jnp.sum(expo, axis=-1, keepdims=True)).astype(jnp.bfloat16)


def onward_kernel(queries, keys, values, rows, tall, wide, out):
    probs = head_probs(queries[...], keys[...], tall[...], wide[...])
    mixed = dot(probs, values[...], ROWS_COLS)
    out[...] = (rows[...].astype(jnp.float32) + mixed).astype(jnp.bfloat16)


def back_kernel(queries, keys, values, grads, tall, wide, query_grad, value_grad, key_part, total):
    head = pl.program_id(0)

    @pl.when(head == 0)
    def _():
        total[...] = jnp.zeros_like(total)

    query, key, grad = queries[...], keys[...], grads[...]
    probs = head_probs(query, key, tall[...], wide[...])
    prob_f = probs.astype(jnp.float32)
    value_grad[...] = dot(probs, grad, FIRST_FIRST)
    prob_grad = dot(grad, values[...], LAST_LAST)
    inner = jnp.sum(prob_grad * prob_f, axis=-1, keepdims=True)
    score_grad = (prob_f * (prob_grad - inner) * HEAD ** (-0.5)).astype(jnp.bfloat16)
    query_grad[...] = dot(score_grad, key, ROWS_COLS).astype(jnp.bfloat16)
    total[...] += dot(score_grad, query, FIRST_FIRST)

    @pl.when(head == pl.num_programs(0) - 1)
    def _():
        key_part[...] = total[...].astype(jnp.bfloat16)


def per_head(kernel, caption, queries, keys, extras, outs, products):
    count, width = queries.shape
    heads = width // HEAD
    by_head = pl.BlockSpec((count, HEAD), lambda h: (0, h))
    fixed = pl.BlockSpec((count, HEAD), lambda h: (0, 0))
    specs = [by_head, fixed] + [by_head] * len(extras)
    specs += [pl.BlockSpec((count, 1), lambda h: (0, 0)), pl.BlockSpec((1, count), lambda h: (0, 0))]
    backward = len(outs) > 1
    return pl.pallas_call(
        kernel,
        grid=(heads,),
        in_specs=specs,
        out_specs=[by_head if shape[1] == width else fixed for shape, kind in outs],
        out_shape=[jax.ShapeDtypeStruct(shape, kind) for shape, kind in outs],
        scratch_shapes=[pltpu.VMEM((count, HEAD), jnp.float32)] if backward else [],
        cost_estimate=pl.CostEstimate(
            flops=2 * products * heads * count * count * HEAD,
            bytes_accessed=2 * (len(extras) + 1 + len(outs)) * count * width,
            transcendentals=heads * count * count,
        ),
        compiler_params=pltpu.CompilerParams(vmem_limit_bytes=24 << 20),
    )(queries, keys, *extras, caption[:, None], caption[None, :])


def updated(weight, step):
    return (weight.astype(jnp.float32) - step.astype(jnp.float32)).astype(jnp.bfloat16)


def halves(mine, theirs):
    return ((mine.astype(jnp.float32) + theirs.astype(jnp.float32)) * 0.5).astype(jnp.bfloat16)


def average_kernel(
    case_ref, scales, weights, slope, slope_other, grad, grad_other, near, above, below, from_up,
    from_down, *rest,
):
    out_ref = rest[-1]
    in_scale = (2 * weights.shape[1]) ** (-0.5)

    def step(rows, cols, scale):
        gradient = dot(rows[...], cols[...], FIRST_FIRST)
        return (gradient * (LEARN_RATE * in_scale * scale)).astype(jnp.bfloat16)

    mine = weights[...] - step(slope, grad, scales[0])
    theirs = step(slope_other, grad_other, scales[1])
    chosen = source_of(pl.program_id(0), case_ref[0])
    for number, weight in enumerate((near, above, below, from_up, from_down)):

        @pl.when(chosen == number)
        def _(weight=weight):
            out_ref[...] = (mine + (weight[...] - theirs)) * 0.5


def source_of(half, case):
    up = jnp.where(case == 1, 4, jnp.where(case == 2, 1, 3))
    down = jnp.where(case == 1, 2, jnp.where(case == 2, 3, 4))
    return jnp.where(case == 0, 0, jnp.where(half == 0, up, down))


def averaged_chunk(case, scales, weights, slopes, grads, near, chunk, cut, out):
    rows, columns = weights.shape
    first, blocks = cut[0] // BLOCK, (cut[1] - cut[0]) // BLOCK
    stride = rows // (2 * BLOCK)

    def whole(half, i, case_ref):
        return (half * stride + first + i, 0)

    def near_map(half, i, case_ref):
        used = source_of(half, case_ref[0]) == 0
        return (jnp.where(used, half * stride + first + i, 0), 0)

    def part_map(number):
        def index(half, i, case_ref):
            return (jnp.where(source_of(half, case_ref[0]) == number, i, 0), 0)

        return index

    block = (BLOCK, columns)
    depth = slopes[0].shape[0]
    in_specs = [pl.BlockSpec(memory_space=pltpu.SMEM), pl.BlockSpec(block, whole)]
    across = pl.BlockSpec((depth, BLOCK), lambda *at: whole(*at)[::-1])
    in_specs += [across] * 2
    in_specs += [pl.BlockSpec((depth, columns), lambda half, i, case_ref: (0, 0))] * 2
    in_specs += [pl.BlockSpec(block, near_map)]
    in_specs += [pl.BlockSpec(block, part_map(number)) for number in range(1, 5)]
    operands = [case.reshape(1), scales, weights, *slopes, *grads, near, *chunk]
    aliases = {}
    if out is not None:
        in_specs.append(pl.BlockSpec(memory_space=pl.ANY))
        aliases = {len(operands): 0}
        operands.append(out)
    size = 2 * blocks * BLOCK * columns
    return pl.pallas_call(
        average_kernel,
        grid_spec=pltpu.PrefetchScalarGridSpec(
            num_scalar_prefetch=1,
            grid=(2, blocks),
            in_specs=in_specs,
            out_specs=pl.BlockSpec(block, whole),
        ),
        out_shape=jax.ShapeDtypeStruct(weights.shape, weights.dtype),
        input_output_aliases=aliases,
        cost_estimate=pl.CostEstimate(
            flops=4 * size * depth, bytes_accessed=6 * size, transcendentals=0
        ),
        compiler_params=pltpu.CompilerParams(vmem_limit_bytes=40 << 20),
    )(*operands)


def settled_kernel(a_ref, b_ref, c_ref, d_ref):
    c_ref[...] = a_ref[...]
    d_ref[...] = b_ref[...]


def settled(a, b):
    block = pl.BlockSpec((64, a.shape[1]), lambda i: (i, 0))
    return pl.pallas_call(
        settled_kernel,
        grid=(a.shape[0] // 64,),
        in_specs=[block, block],
        out_specs=[block, block],
        out_shape=[jax.ShapeDtypeStruct(x.shape, x.dtype) for x in (a, b)],
        cost_estimate=pl.CostEstimate(flops=0, bytes_accessed=8 * a.size, transcendentals=0),
        compiler_params=pltpu.CompilerParams(vmem_limit_bytes=8 << 20),
    )(a, b)


def section(fwd_in, bwd_in, bwd_grad, seg_fwd, seg_bwd, w_query, w_key, gain, gossip_exp):
    query_weight = w_query[0, 0]
    key_weight = w_key[0, 0]
    gain_local = gain[0, 0]
    fwd_rows = fwd_in[0, 0]
    bwd_rows = bwd_in[0, 0]
    grad_rows = bwd_grad[0, 0]
    count, local_width = fwd_rows.shape
    tp_count = lax.axis_size("tp")
    pipe_count = lax.axis_size("pipe")
    tp_index = lax.axis_index("tp")
    low = tp_index == 0
    offset = tp_index * local_width
    gossip = Gossip(gossip_exp[0])

    beside = jnp.broadcast_to(gain_local[None], (16, local_width))
    other = flipped(jnp.concatenate([bwd_rows, beside], axis=0), "tp", 0)
    bwd_full = in_order(bwd_rows, other[:count], low, 1)
    gain_full = in_order(gain_local, other[count], low, 0)
    width = bwd_full.shape[1]
    in_scale = width ** (-0.5)

    cuts = chunk_cuts(width // 2)
    parts = [
        [query_weight[base + a : base + b] for a, b in cuts] for base in (0, width // 2)
    ]
    sent = []
    for up, down in zip(*parts):
        sent.append(gossip.first(up, down))
    query_near = flipped(query_weight, "rep", 0)

    _, scaled_b, inv_b, normed_b = normalize(bwd_full, gain_full)
    own_values_b = lax.dynamic_slice_in_dim(normed_b, offset, local_width, 1)
    key_rows = lax.dynamic_slice_in_dim(key_weight, offset, local_width, 0)
    early = gossip.small(
        jnp.concatenate([own_values_b, key_rows.reshape(HEAD, local_width)], axis=0)
    )
    early_other = flipped(early, "tp", 0)
    normed_partner = in_order(early[:count], early_other[:count], low, 1)
    key_partner = in_order(
        early[count:].reshape(local_width, HEAD),
        early_other[count:].reshape(local_width, HEAD),
        low,
        0,
    )

    queries = projected(normed_b, query_weight)
    keys = projected(normed_b, key_weight)
    query_grad, value_grad, key_part = per_head(
        back_kernel,
        seg_bwd[0, 0],
        queries,
        keys,
        (own_values_b, grad_rows),
        (
            ((count, local_width), jnp.bfloat16),
            ((count, local_width), jnp.float32),
            ((count, HEAD), jnp.bfloat16),
        ),
        5,
    )

    def tp_sum(part):
        other = flipped(part, "tp", 0)
        return (part.astype(jnp.float32) + other.astype(jnp.float32)).astype(jnp.bfloat16)

    late = gossip.small(jnp.concatenate([query_grad, key_part], axis=1))
    query_grad_partner = late[:, :local_width]
    key_grad = tp_sum(key_part)
    key_grad_partner = tp_sum(late[:, local_width:])

    contract_last = (((1,), (1,)), ((), ()))
    partial_grad = (
        lax.dot_general(query_grad, query_weight, contract_last, preferred_element_type=jnp.float32)
        * in_scale
    )
    own_part = (lax.dynamic_slice_in_dim(partial_grad, offset, local_width, 1) + value_grad).astype(
        jnp.bfloat16
    )
    other_part = lax.dynamic_slice_in_dim(
        partial_grad, local_width - offset, local_width, 1
    ).astype(jnp.bfloat16)
    from_other = flipped(other_part, "tp", 0)
    full_grad = (
        own_part.astype(jnp.float32)
        + from_other.astype(jnp.float32)
        + lax.dot_general(key_grad, key_rows, contract_last, preferred_element_type=jnp.float32)
        * in_scale
    )
    own_scaled = lax.dynamic_slice_in_dim(scaled_b, offset, local_width, 1)
    weighted = full_grad * gain_local.astype(jnp.float32)
    sums = jnp.stack([jnp.sum(weighted, axis=-1), jnp.sum(weighted * own_scaled, axis=-1)])
    means = (sums + flipped(sums, "tp", 0)) / width
    input_grad = inv_b * (weighted - means[0][:, None] - own_scaled * means[1][:, None])
    grad_gain = jnp.sum(full_grad * own_scaled, axis=0)
    back_rows = (grad_rows.astype(jnp.float32) + input_grad).astype(jnp.bfloat16)
    prev_rows = from_behind(back_rows, "pipe", -1)

    contract_first = (((0,), (0,)), ((), ()))

    def weight_grad(rows, grad):
        return (
            lax.dot_general(rows, grad, contract_first, preferred_element_type=jnp.float32)
            * in_scale
        )

    grad_query = weight_grad(normed_b, query_grad)
    query_squares = jnp.sum(grad_query * grad_query)
    grad_key = weight_grad(normed_b, key_grad)
    local_squares = (
        query_squares
        + jnp.sum(grad_gain * grad_gain)
        + jnp.sum(grad_key * grad_key) / tp_count
    )
    fwd_other, local_squares = lax.optimization_barrier(
        (flipped(fwd_rows, "tp", 0), local_squares)
    )
    fwd_full = in_order(fwd_rows, fwd_other, low, 1)
    _, _, _, normed = normalize(fwd_full, gain_full)
    own_values = lax.dynamic_slice_in_dim(normed, offset, local_width, 1)
    queries_f = projected(normed, query_weight)
    keys_f = projected(normed, key_weight)
    (section_out,) = per_head(
        onward_kernel,
        seg_fwd[0, 0],
        queries_f,
        keys_f,
        (own_values, fwd_rows),
        (((count, local_width), jnp.bfloat16),),
        2,
    )
    next_rows = from_behind(section_out, "pipe", 1)

    total_squares = of_everyone(local_squares, ("pipe", "tp"))
    total = pipe_count * (width * width + width * HEAD + width)
    inverse = lax.rsqrt(total_squares / total + STEP_EPS)

    def step_of(gradient, scale):
        return (LEARN_RATE * gradient * scale).astype(jnp.bfloat16)

    gain_new = updated(gain_local, step_of(grad_gain, inverse))
    both = gossip.tiny(
        jnp.concatenate([gain_new.astype(jnp.float32), jnp.broadcast_to(inverse, (HEAD,))])
    )
    gain_partner = both[:local_width].astype(jnp.bfloat16)
    inverse_partner = both[local_width]
    gain_out = halves(gain_new, gain_partner)

    key_out = halves(
        updated(key_weight, step_of(grad_key, inverse)),
        updated(
            key_partner,
            step_of(weight_grad(normed_partner, key_grad_partner), inverse_partner),
        ),
    )
    later = []
    for state in sent:
        later.append(gossip.second(state))
    next_rows, prev_rows = settled(next_rows, prev_rows)
    slopes = (normed_b, normed_partner)
    query_out = None
    for i, cut in enumerate(cuts):
        query_out = averaged_chunk(
            gossip.case,
            jnp.stack([inverse, inverse_partner]),
            query_weight,
            slopes,
            (query_grad, query_grad_partner),
            query_near,
            later[i],
            cut,
            query_out,
        )
    return (
        next_rows[None, None],
        prev_rows[None, None],
        query_out[None, None],
        key_out[None, None],
        gain_out[None, None],
    )


def solution(mesh):
    return jax.shard_map(
        section,
        mesh=mesh,
        in_specs=(
            P("rep", "pipe", None, "tp"),
            P("rep", "pipe", None, "tp"),
            P("rep", "pipe", None, "tp"),
            P("rep", "pipe", None),
            P("rep", "pipe", None),
            P("rep", "pipe", None, "tp"),
            P("rep", "pipe", None, None),
            P("rep", "pipe", "tp"),
            P("pipe"),
        ),
        out_specs=(
            P("rep", "pipe", None, "tp"),
            P("rep", "pipe", None, "tp"),
            P("rep", "pipe", None, "tp"),
            P("rep", "pipe", None, None),
            P("rep", "pipe", "tp"),
        ),
        check_vma=False,
    )
```

```python
import jax
import jax.numpy as jnp
from jax import lax
from jax.experimental import pallas as pl
from jax.experimental.pallas import tpu as pltpu
from jax.sharding import PartitionSpec as P


HEAD = 128


LN_EPS = 1e-05
STEP_EPS = 1e-06
LEARN_RATE = 0.2
MASK_FILL = -1e30
CHUNK_SHARES = (2, 3, 1)
BLOCK = 256
STRIP = 512


def from_behind(shard, axis, by):
    length = lax.axis_size(axis)
    return lax.ppermute(shard, axis, [(i, (i + by) % length) for i in range(length)])


def flipped(block, axis, bit):
    return lax.ppermute(block, axis, [(i, i ^ 1 << bit) for i in range(lax.axis_size(axis))])


def in_order(own, other, low, axis):
    return jnp.where(
        low, jnp.concatenate([own, other], axis), jnp.concatenate([other, own], axis)
    )


def of_everyone(shard, axis):
    copies = jnp.broadcast_to(shard, (lax.axis_size(axis), *shard.shape))
    return jnp.sum(lax.all_to_all(copies, axis, split_axis=0, concat_axis=0, tiled=True), axis=0)


def chunk_cuts(rows):
    whole, edges = sum(CHUNK_SHARES), [0]
    for share in CHUNK_SHARES:
        edges.append(edges[-1] + rows * share // whole)
    return list(zip(edges[:-1], edges[1:]))


def relay_kernel(case_ref, up, down, above_in, below_in, above, below, held, sem):
    def carry(source, target):
        for one, other in ((source, held), (held, target)):
            copy = pltpu.make_async_copy(one, other, sem)
            copy.start()
            copy.wait()

    @pl.when(case_ref[0] == 1)
    def _():
        carry(down, above)

    @pl.when(case_ref[0] == 2)
    def _():
        carry(up, below)


def relayed(case, up, down, above, below):
    anywhere = pl.BlockSpec(memory_space=pl.ANY)
    return pl.pallas_call(
        relay_kernel,
        in_specs=[pl.BlockSpec(memory_space=pltpu.SMEM)] + [anywhere] * 4,
        out_specs=[anywhere] * 2,
        out_shape=[jax.ShapeDtypeStruct(up.shape, up.dtype)] * 2,
        input_output_aliases={3: 0, 4: 1},
        scratch_shapes=[pltpu.VMEM(up.shape, up.dtype), pltpu.SemaphoreType.DMA],
        cost_estimate=pl.CostEstimate(flops=0, bytes_accessed=up.size, transcendentals=0),
        compiler_params=pltpu.CompilerParams(vmem_limit_bytes=8 << 20),
    )(case.reshape(1), up, down, above, below)


class Gossip:
    def __init__(self, exponent):
        self.exponent = exponent
        odd = (lax.axis_index("rep") // 2) % 2
        self.case = jnp.where(exponent == 2, 3, jnp.where(exponent == 1, 1 + odd, 0))

    def first(self, up, down):
        return up, down, from_behind(up, "rep", 2), from_behind(down, "rep", -2)

    def second(self, state):
        above, below = relayed(self.case, *state)
        return above, below, from_behind(above, "rep", 2), from_behind(below, "rep", -2)

    def small(self, block):
        half = block.shape[0] // 2
        up, down, block = lax.optimization_barrier((block[:half], block[half:], block))
        state = self.first(up, down)
        above, below, from_up, from_down = self.second(state)
        near = flipped(block, "rep", 0)
        case = self.case

        def pick(a, b, c, d):
            return jnp.where(case == 0, a, jnp.where(case == 1, b, jnp.where(case == 2, c, d)))

        return jnp.concatenate(
            [
                pick(near[:half], from_down, above, from_up),
                pick(near[half:], below, from_up, from_down),
            ],
            axis=0,
        )

    def tiny(self, block):
        results = [flipped(block, "rep", bit) for bit in range(3)]
        return jnp.where(
            self.exponent == 0, results[0], jnp.where(self.exponent == 1, results[1], results[2])
        )


def normalize(rows, gain_full):
    values = rows.astype(jnp.float32)
    centred = values - jnp.mean(values, axis=-1, keepdims=True)
    inv_std = lax.rsqrt(jnp.mean(centred * centred, axis=-1, keepdims=True) + LN_EPS)
    scaled = centred * inv_std
    normed = (scaled * gain_full.astype(jnp.float32)).astype(jnp.bfloat16)
    return (values, scaled, inv_std, normed)


def projected(normed, weight):
    in_scale = normed.shape[1] ** (-0.5)
    product = jnp.dot(normed, weight, preferred_element_type=jnp.float32)
    return (product * in_scale).astype(jnp.bfloat16)


def dot(a, b, over):
    return lax.dot_general(a, b, (over, ((), ())), preferred_element_type=jnp.float32)


ROWS_COLS, LAST_LAST, FIRST_FIRST = ((1,), (0,)), ((1,), (1,)), ((0,), (0,))


def head_probs(queries, keys, tall, wide):
    scores = dot(queries, keys, LAST_LAST) * HEAD ** (-0.5)
    scores = jnp.where(tall == wide, scores, MASK_FILL)
    peak = jnp.max(scores, axis=-1, keepdims=True)
    expo = jnp.exp(scores - peak)
    return (expo / jnp.sum(expo, axis=-1, keepdims=True)).astype(jnp.bfloat16)


def onward_kernel(queries, keys, values, rows, tall, wide, out):
    probs = head_probs(queries[...], keys[...], tall[...], wide[...])
    mixed = dot(probs, values[...], ROWS_COLS)
    out[...] = (rows[...].astype(jnp.float32) + mixed).astype(jnp.bfloat16)


def back_kernel(queries, keys, values, grads, tall, wide, query_grad, value_grad, key_part, total):
    head = pl.program_id(0)

    @pl.when(head == 0)
    def _():
        total[...] = jnp.zeros_like(total)

    query, key, grad = queries[...], keys[...], grads[...]
    probs = head_probs(query, key, tall[...], wide[...])
    prob_f = probs.astype(jnp.float32)
    value_grad[...] = dot(probs, grad, FIRST_FIRST)
    prob_grad = dot(grad, values[...], LAST_LAST)
    inner = jnp.sum(prob_grad * prob_f, axis=-1, keepdims=True)
    score_grad = (prob_f * (prob_grad - inner) * HEAD ** (-0.5)).astype(jnp.bfloat16)
    query_grad[...] = dot(score_grad, key, ROWS_COLS).astype(jnp.bfloat16)
    total[...] += dot(score_grad, query, FIRST_FIRST)

    @pl.when(head == pl.num_programs(0) - 1)
    def _():
        key_part[...] = total[...].astype(jnp.bfloat16)


def per_head(kernel, caption, queries, keys, extras, outs, products):
    count, width = queries.shape
    heads = width // HEAD
    by_head = pl.BlockSpec((count, HEAD), lambda h: (0, h))
    fixed = pl.BlockSpec((count, HEAD), lambda h: (0, 0))
    specs = [by_head, fixed] + [by_head] * len(extras)
    specs += [pl.BlockSpec((count, 1), lambda h: (0, 0)), pl.BlockSpec((1, count), lambda h: (0, 0))]
    backward = len(outs) > 1
    return pl.pallas_call(
        kernel,
        grid=(heads,),
        in_specs=specs,
        out_specs=[by_head if shape[1] == width else fixed for shape, kind in outs],
        out_shape=[jax.ShapeDtypeStruct(shape, kind) for shape, kind in outs],
        scratch_shapes=[pltpu.VMEM((count, HEAD), jnp.float32)] if backward else [],
        cost_estimate=pl.CostEstimate(
            flops=2 * products * heads * count * count * HEAD,
            bytes_accessed=2 * (len(extras) + 1 + len(outs)) * count * width,
            transcendentals=heads * count * count,
        ),
        compiler_params=pltpu.CompilerParams(vmem_limit_bytes=24 << 20),
    )(queries, keys, *extras, caption[:, None], caption[None, :])


def updated(weight, step):
    return (weight.astype(jnp.float32) - step.astype(jnp.float32)).astype(jnp.bfloat16)


def halves(mine, theirs):
    return ((mine.astype(jnp.float32) + theirs.astype(jnp.float32)) * 0.5).astype(jnp.bfloat16)


def average_kernel(
    case_ref, scales, weights, slope, slope_other, grad, grad_other, near, above, below, from_up,
    from_down, *rest,
):
    out_ref = rest[-1]
    columns = weights.shape[1]
    in_scale = (2 * columns) ** (-0.5)
    flipped_own, flipped_other = slope[...].T, slope_other[...].T
    chosen = source_of(pl.program_id(0), case_ref[0])

    def strip(number, carry):
        cols = pl.ds(pl.multiple_of(number * STRIP, STRIP), STRIP)

        def step(rows, grads, scale):
            gradient = dot(rows, grads[:, cols], ROWS_COLS)
            return (gradient * (LEARN_RATE * in_scale * scale)).astype(jnp.bfloat16)

        mine = weights[:, cols] - step(flipped_own, grad, scales[0])
        theirs = step(flipped_other, grad_other, scales[1])
        partner = near[:, cols]
        for source, weight in enumerate((above, below, from_up, from_down), 1):
            partner = jnp.where(chosen == source, weight[:, cols], partner)
        out_ref[:, cols] = (mine + (partner - theirs)) * 0.5
        return carry

    lax.fori_loop(0, columns // STRIP, strip, 0)


def squares_kernel(slope, grad, key_grad, out, total):
    step = pl.program_id(0)

    @pl.when(step == 0)
    def _():
        total[...] = jnp.zeros_like(total)

    rows = slope[...].T
    columns = grad.shape[1]

    def added(grads):
        gradient = dot(rows, grads, ROWS_COLS)
        return jnp.sum((gradient * gradient).reshape(-1, 8, gradient.shape[1]), axis=0)

    def strip(number, carry):
        cols = pl.ds(pl.multiple_of(number * STRIP, STRIP), STRIP)
        total[...] += added(grad[:, cols])
        return carry

    lax.fori_loop(0, columns // STRIP, strip, 0)
    total[:, :HEAD] += added(key_grad[...]) * 0.5

    @pl.when(step == pl.num_programs(0) - 1)
    def _():
        out[...] = jnp.sum(total[...], keepdims=True)


def gradient_squares(slope, grad, key_grad):
    depth, rows = slope.shape
    in_scale = rows ** (-0.5)
    size = rows * (grad.shape[1] + HEAD) * depth
    block = rows // 3
    squares = pl.pallas_call(
        squares_kernel,
        grid=(rows // block,),
        in_specs=[
            pl.BlockSpec((depth, block), lambda i: (0, i)),
            pl.BlockSpec(grad.shape, lambda i: (0, 0)),
            pl.BlockSpec(key_grad.shape, lambda i: (0, 0)),
        ],
        out_specs=pl.BlockSpec((1, 1), lambda i: (0, 0)),
        out_shape=jax.ShapeDtypeStruct((1, 1), jnp.float32),
        scratch_shapes=[pltpu.VMEM((8, STRIP), jnp.float32)],
        cost_estimate=pl.CostEstimate(
            flops=2 * size, bytes_accessed=2 * slope.size + 2 * grad.size, transcendentals=0
        ),
        compiler_params=pltpu.CompilerParams(vmem_limit_bytes=16 << 20),
    )(slope, grad, key_grad)
    return squares[0, 0] * (in_scale * in_scale)


def source_of(half, case):
    up = jnp.where(case == 1, 4, jnp.where(case == 2, 1, 3))
    down = jnp.where(case == 1, 2, jnp.where(case == 2, 3, 4))
    return jnp.where(case == 0, 0, jnp.where(half == 0, up, down))


def averaged_chunk(case, scales, weights, slopes, grads, near, chunk, cut, out):
    rows, columns = weights.shape
    first, blocks = cut[0] // BLOCK, (cut[1] - cut[0]) // BLOCK
    stride = rows // (2 * BLOCK)

    def whole(half, i, case_ref):
        return (half * stride + first + i, 0)

    def near_map(half, i, case_ref):
        used = source_of(half, case_ref[0]) == 0
        return (jnp.where(used, half * stride + first + i, 0), 0)

    def part_map(number):
        def index(half, i, case_ref):
            return (jnp.where(source_of(half, case_ref[0]) == number, i, 0), 0)

        return index

    block = (BLOCK, columns)
    depth = slopes[0].shape[0]
    in_specs = [pl.BlockSpec(memory_space=pltpu.SMEM), pl.BlockSpec(block, whole)]
    across = pl.BlockSpec((depth, BLOCK), lambda *at: whole(*at)[::-1])
    in_specs += [across] * 2
    in_specs += [pl.BlockSpec((depth, columns), lambda half, i, case_ref: (0, 0))] * 2
    in_specs += [pl.BlockSpec(block, near_map)]
    in_specs += [pl.BlockSpec(block, part_map(number)) for number in range(1, 5)]
    operands = [case.reshape(1), scales, weights, *slopes, *grads, near, *chunk]
    aliases = {}
    if out is not None:
        in_specs.append(pl.BlockSpec(memory_space=pl.ANY))
        aliases = {len(operands): 0}
        operands.append(out)
    size = 2 * blocks * BLOCK * columns
    return pl.pallas_call(
        average_kernel,
        grid_spec=pltpu.PrefetchScalarGridSpec(
            num_scalar_prefetch=1,
            grid=(2, blocks),
            in_specs=in_specs,
            out_specs=pl.BlockSpec(block, whole),
        ),
        out_shape=jax.ShapeDtypeStruct(weights.shape, weights.dtype),
        input_output_aliases=aliases,
        cost_estimate=pl.CostEstimate(
            flops=4 * size * depth, bytes_accessed=6 * size, transcendentals=0
        ),
        compiler_params=pltpu.CompilerParams(vmem_limit_bytes=40 << 20),
    )(*operands)


def settled_kernel(a_ref, b_ref, c_ref, d_ref):
    c_ref[...] = a_ref[...]
    d_ref[...] = b_ref[...]


def settled(a, b):
    block = pl.BlockSpec((64, a.shape[1]), lambda i: (i, 0))
    return pl.pallas_call(
        settled_kernel,
        grid=(a.shape[0] // 64,),
        in_specs=[block, block],
        out_specs=[block, block],
        out_shape=[jax.ShapeDtypeStruct(x.shape, x.dtype) for x in (a, b)],
        cost_estimate=pl.CostEstimate(flops=0, bytes_accessed=8 * a.size, transcendentals=0),
        compiler_params=pltpu.CompilerParams(vmem_limit_bytes=8 << 20),
    )(a, b)


def section(fwd_in, bwd_in, bwd_grad, seg_fwd, seg_bwd, w_query, w_key, gain, gossip_exp):
    query_weight = w_query[0, 0]
    key_weight = w_key[0, 0]
    gain_local = gain[0, 0]
    fwd_rows = fwd_in[0, 0]
    bwd_rows = bwd_in[0, 0]
    grad_rows = bwd_grad[0, 0]
    count, local_width = fwd_rows.shape
    pipe_count = lax.axis_size("pipe")
    tp_index = lax.axis_index("tp")
    low = tp_index == 0
    offset = tp_index * local_width
    gossip = Gossip(gossip_exp[0])

    width = query_weight.shape[0]
    in_scale = width ** (-0.5)
    cuts = chunk_cuts(width // 2)
    parts = [
        [query_weight[base + a : base + b] for a, b in cuts] for base in (0, width // 2)
    ]
    sent = []
    for up, down in zip(*parts):
        sent.append(gossip.first(up, down))
    query_near = flipped(query_weight, "rep", 0)

    beside = jnp.broadcast_to(gain_local[None], (16, local_width))
    other = flipped(jnp.concatenate([bwd_rows, beside], axis=0), "tp", 0)
    bwd_full = in_order(bwd_rows, other[:count], low, 1)
    gain_full = in_order(gain_local, other[count], low, 0)

    _, scaled_b, inv_b, normed_b = normalize(bwd_full, gain_full)
    own_values_b = lax.dynamic_slice_in_dim(normed_b, offset, local_width, 1)
    key_rows = lax.dynamic_slice_in_dim(key_weight, offset, local_width, 0)
    early = gossip.small(
        jnp.concatenate([own_values_b, key_rows.reshape(HEAD, local_width)], axis=0)
    )
    early_other = flipped(early, "tp", 0)
    normed_partner = in_order(early[:count], early_other[:count], low, 1)
    key_partner = in_order(
        early[count:].reshape(local_width, HEAD),
        early_other[count:].reshape(local_width, HEAD),
        low,
        0,
    )

    queries = projected(normed_b, query_weight)
    keys = projected(normed_b, key_weight)
    query_grad, value_grad, key_part = per_head(
        back_kernel,
        seg_bwd[0, 0],
        queries,
        keys,
        (own_values_b, grad_rows),
        (
            ((count, local_width), jnp.bfloat16),
            ((count, local_width), jnp.float32),
            ((count, HEAD), jnp.bfloat16),
        ),
        5,
    )

    def tp_sum(part):
        other = flipped(part, "tp", 0)
        return (part.astype(jnp.float32) + other.astype(jnp.float32)).astype(jnp.bfloat16)

    late = gossip.small(jnp.concatenate([query_grad, key_part], axis=1))
    query_grad_partner = late[:, :local_width]
    key_grad = tp_sum(key_part)
    key_grad_partner = tp_sum(late[:, local_width:])

    contract_last = (((1,), (1,)), ((), ()))
    partial_grad = (
        lax.dot_general(query_grad, query_weight, contract_last, preferred_element_type=jnp.float32)
        * in_scale
    )
    own_part = (lax.dynamic_slice_in_dim(partial_grad, offset, local_width, 1) + value_grad).astype(
        jnp.bfloat16
    )
    other_part = lax.dynamic_slice_in_dim(
        partial_grad, local_width - offset, local_width, 1
    ).astype(jnp.bfloat16)
    from_other = flipped(other_part, "tp", 0)
    full_grad = (
        own_part.astype(jnp.float32)
        + from_other.astype(jnp.float32)
        + lax.dot_general(key_grad, key_rows, contract_last, preferred_element_type=jnp.float32)
        * in_scale
    )
    own_scaled = lax.dynamic_slice_in_dim(scaled_b, offset, local_width, 1)
    weighted = full_grad * gain_local.astype(jnp.float32)
    sums = jnp.stack([jnp.sum(weighted, axis=-1), jnp.sum(weighted * own_scaled, axis=-1)])
    means = (sums + flipped(sums, "tp", 0)) / width
    input_grad = inv_b * (weighted - means[0][:, None] - own_scaled * means[1][:, None])
    grad_gain = jnp.sum(full_grad * own_scaled, axis=0)
    back_rows = (grad_rows.astype(jnp.float32) + input_grad).astype(jnp.bfloat16)
    prev_rows = from_behind(back_rows, "pipe", -1)

    contract_first = (((0,), (0,)), ((), ()))

    def weight_grad(rows, grad):
        return (
            lax.dot_general(rows, grad, contract_first, preferred_element_type=jnp.float32)
            * in_scale
        )

    query_squares = gradient_squares(normed_b, query_grad, key_grad)
    grad_key = weight_grad(normed_b, key_grad)
    local_squares = query_squares + jnp.sum(grad_gain * grad_gain)
    fwd_other = flipped(fwd_rows, "tp", 0)
    fwd_other, local_squares = lax.optimization_barrier((fwd_other, local_squares))
    fwd_full = in_order(fwd_rows, fwd_other, low, 1)
    _, _, _, normed = normalize(fwd_full, gain_full)
    own_values = lax.dynamic_slice_in_dim(normed, offset, local_width, 1)
    queries_f = projected(normed, query_weight)
    keys_f = projected(normed, key_weight)
    (section_out,) = per_head(
        onward_kernel,
        seg_fwd[0, 0],
        queries_f,
        keys_f,
        (own_values, fwd_rows),
        (((count, local_width), jnp.bfloat16),),
        2,
    )
    next_rows = from_behind(section_out, "pipe", 1)

    total_squares = of_everyone(local_squares, ("pipe", "tp"))
    total = pipe_count * (width * width + width * HEAD + width)
    inverse = lax.rsqrt(total_squares / total + STEP_EPS)

    def step_of(gradient, scale):
        return (LEARN_RATE * gradient * scale).astype(jnp.bfloat16)

    gain_new = updated(gain_local, step_of(grad_gain, inverse))
    both = gossip.tiny(
        jnp.concatenate([gain_new.astype(jnp.float32), jnp.broadcast_to(inverse, (HEAD,))])
    )
    gain_partner = both[:local_width].astype(jnp.bfloat16)
    inverse_partner = both[local_width]
    gain_out = halves(gain_new, gain_partner)

    key_out = halves(
        updated(key_weight, step_of(grad_key, inverse)),
        updated(
            key_partner,
            step_of(weight_grad(normed_partner, key_grad_partner), inverse_partner),
        ),
    )
    later = []
    for state in sent:
        later.append(gossip.second(state))
    next_rows, prev_rows = settled(next_rows, prev_rows)
    slopes = (normed_b, normed_partner)
    query_out = None
    for i, cut in enumerate(cuts):
        query_out = averaged_chunk(
            gossip.case,
            jnp.stack([inverse, inverse_partner]),
            query_weight,
            slopes,
            (query_grad, query_grad_partner),
            query_near,
            later[i],
            cut,
            query_out,
        )
    return (
        next_rows[None, None],
        prev_rows[None, None],
        query_out[None, None],
        key_out[None, None],
        gain_out[None, None],
    )


def solution(mesh):
    return jax.shard_map(
        section,
        mesh=mesh,
        in_specs=(
            P("rep", "pipe", None, "tp"),
            P("rep", "pipe", None, "tp"),
            P("rep", "pipe", None, "tp"),
            P("rep", "pipe", None),
            P("rep", "pipe", None),
            P("rep", "pipe", None, "tp"),
            P("rep", "pipe", None, None),
            P("rep", "pipe", "tp"),
            P("pipe"),
        ),
        out_specs=(
            P("rep", "pipe", None, "tp"),
            P("rep", "pipe", None, "tp"),
            P("rep", "pipe", None, "tp"),
            P("rep", "pipe", None, None),
            P("rep", "pipe", "tp"),
        ),
        check_vma=False,
    )
```

```python
from functools import partial

import jax
import jax.numpy as jnp
from jax import lax
from jax.experimental import pallas as pl
from jax.experimental.pallas import tpu as pltpu
from jax.sharding import PartitionSpec as P


HEAD = 128


LN_EPS = 1e-05
STEP_EPS = 1e-06
LEARN_RATE = 0.2
MASK_FILL = -1e30
BLOCK = 256
STRIP = 512


def from_behind(shard, axis, by):
    length = lax.axis_size(axis)
    return lax.ppermute(shard, axis, [(i, (i + by) % length) for i in range(length)])


def flipped(block, axis, bit):
    return lax.ppermute(block, axis, [(i, i ^ 1 << bit) for i in range(lax.axis_size(axis))])


def in_order(own, other, low, axis):
    return jnp.where(
        low, jnp.concatenate([own, other], axis), jnp.concatenate([other, own], axis)
    )


def of_everyone(shard, axis):
    copies = jnp.broadcast_to(shard, (lax.axis_size(axis), *shard.shape))
    return jnp.sum(lax.all_to_all(copies, axis, split_axis=0, concat_axis=0, tiled=True), axis=0)


def relay_kernel(case_ref, up, down, above_in, below_in, above, below, held, sem):
    def carry(source, target):
        for one, other in ((source, held), (held, target)):
            copy = pltpu.make_async_copy(one, other, sem)
            copy.start()
            copy.wait()

    @pl.when(case_ref[0] == 1)
    def _():
        carry(down, above)

    @pl.when(case_ref[0] == 2)
    def _():
        carry(up, below)


def relayed(case, up, down, above, below):
    anywhere = pl.BlockSpec(memory_space=pl.ANY)
    return pl.pallas_call(
        relay_kernel,
        in_specs=[pl.BlockSpec(memory_space=pltpu.SMEM)] + [anywhere] * 4,
        out_specs=[anywhere] * 2,
        out_shape=[jax.ShapeDtypeStruct(up.shape, up.dtype)] * 2,
        input_output_aliases={3: 0, 4: 1},
        scratch_shapes=[pltpu.VMEM(up.shape, up.dtype), pltpu.SemaphoreType.DMA],
        cost_estimate=pl.CostEstimate(flops=0, bytes_accessed=up.size, transcendentals=0),
        compiler_params=pltpu.CompilerParams(vmem_limit_bytes=8 << 20),
    )(case.reshape(1), up, down, above, below)


class Gossip:
    def __init__(self, exponent):
        self.exponent = exponent
        odd = (lax.axis_index("rep") // 2) % 2
        self.case = jnp.where(exponent == 2, 3, jnp.where(exponent == 1, 1 + odd, 0))

    def first(self, up, down):
        return up, down, from_behind(up, "rep", 2), from_behind(down, "rep", -2)

    def second(self, state):
        above, below = relayed(self.case, *state)
        return above, below, from_behind(above, "rep", 2), from_behind(below, "rep", -2)

    def small(self, block):
        half = block.shape[0] // 2
        up, down, block = lax.optimization_barrier((block[:half], block[half:], block))
        state = self.first(up, down)
        above, below, from_up, from_down = self.second(state)
        near = flipped(block, "rep", 0)
        case = self.case

        def pick(a, b, c, d):
            return jnp.where(case == 0, a, jnp.where(case == 1, b, jnp.where(case == 2, c, d)))

        return jnp.concatenate(
            [
                pick(near[:half], from_down, above, from_up),
                pick(near[half:], below, from_up, from_down),
            ],
            axis=0,
        )

    def tiny(self, block):
        results = [flipped(block, "rep", bit) for bit in range(3)]
        return jnp.where(
            self.exponent == 0, results[0], jnp.where(self.exponent == 1, results[1], results[2])
        )


def normalize(rows, gain_full):
    values = rows.astype(jnp.float32)
    centred = values - jnp.mean(values, axis=-1, keepdims=True)
    inv_std = lax.rsqrt(jnp.mean(centred * centred, axis=-1, keepdims=True) + LN_EPS)
    scaled = centred * inv_std
    normed = (scaled * gain_full.astype(jnp.float32)).astype(jnp.bfloat16)
    return (values, scaled, inv_std, normed)


def projected(normed, weight):
    in_scale = normed.shape[1] ** (-0.5)
    product = jnp.dot(normed, weight, preferred_element_type=jnp.float32)
    return (product * in_scale).astype(jnp.bfloat16)


def dot(a, b, over):
    return lax.dot_general(a, b, (over, ((), ())), preferred_element_type=jnp.float32)


ROWS_COLS, LAST_LAST, FIRST_FIRST = ((1,), (0,)), ((1,), (1,)), ((0,), (0,))


def head_probs(queries, keys, tall, wide):
    scores = dot(queries, keys, LAST_LAST) * HEAD ** (-0.5)
    scores = jnp.where(tall == wide, scores, MASK_FILL)
    peak = jnp.max(scores, axis=-1, keepdims=True)
    expo = jnp.exp(scores - peak)
    return (expo / jnp.sum(expo, axis=-1, keepdims=True)).astype(jnp.bfloat16)


def onward_kernel(queries, keys, values, rows, tall, wide, out):
    probs = head_probs(queries[...], keys[...], tall[...], wide[...])
    mixed = dot(probs, values[...], ROWS_COLS)
    out[...] = (rows[...].astype(jnp.float32) + mixed).astype(jnp.bfloat16)


def back_kernel(queries, keys, values, grads, tall, wide, query_grad, value_grad, key_part, total):
    head = pl.program_id(0)

    @pl.when(head == 0)
    def _():
        total[...] = jnp.zeros_like(total)

    query, key, grad = queries[...], keys[...], grads[...]
    probs = head_probs(query, key, tall[...], wide[...])
    prob_f = probs.astype(jnp.float32)
    value_grad[...] = dot(probs, grad, FIRST_FIRST)
    prob_grad = dot(grad, values[...], LAST_LAST)
    inner = jnp.sum(prob_grad * prob_f, axis=-1, keepdims=True)
    score_grad = (prob_f * (prob_grad - inner) * HEAD ** (-0.5)).astype(jnp.bfloat16)
    query_grad[...] = dot(score_grad, key, ROWS_COLS).astype(jnp.bfloat16)
    total[...] += dot(score_grad, query, FIRST_FIRST)

    @pl.when(head == pl.num_programs(0) - 1)
    def _():
        key_part[...] = total[...].astype(jnp.bfloat16)


def per_head(kernel, caption, queries, keys, extras, outs, products):
    count, width = queries.shape
    heads = width // HEAD
    by_head = pl.BlockSpec((count, HEAD), lambda h: (0, h))
    fixed = pl.BlockSpec((count, HEAD), lambda h: (0, 0))
    specs = [by_head, fixed] + [by_head] * len(extras)
    specs += [pl.BlockSpec((count, 1), lambda h: (0, 0)), pl.BlockSpec((1, count), lambda h: (0, 0))]
    backward = len(outs) > 1
    return pl.pallas_call(
        kernel,
        grid=(heads,),
        in_specs=specs,
        out_specs=[by_head if shape[1] == width else fixed for shape, kind in outs],
        out_shape=[jax.ShapeDtypeStruct(shape, kind) for shape, kind in outs],
        scratch_shapes=[pltpu.VMEM((count, HEAD), jnp.float32)] if backward else [],
        cost_estimate=pl.CostEstimate(
            flops=2 * products * heads * count * count * HEAD,
            bytes_accessed=2 * (len(extras) + 1 + len(outs)) * count * width,
            transcendentals=heads * count * count,
        ),
        compiler_params=pltpu.CompilerParams(vmem_limit_bytes=24 << 20),
    )(queries, keys, *extras, caption[:, None], caption[None, :])


def updated(weight, step):
    return (weight.astype(jnp.float32) - step.astype(jnp.float32)).astype(jnp.bfloat16)


def halves(mine, theirs):
    return ((mine.astype(jnp.float32) + theirs.astype(jnp.float32)) * 0.5).astype(jnp.bfloat16)


def strips(columns, body):
    def at(number, carry):
        body(pl.ds(pl.multiple_of(number * STRIP, STRIP), STRIP))
        return carry

    lax.fori_loop(0, columns // STRIP, at, 0)


def stepped(rows, grads, scale):
    in_scale = (2 * grads.shape[1]) ** (-0.5)

    def at(cols):
        gradient = dot(rows, grads[:, cols], ROWS_COLS)
        return (gradient * (LEARN_RATE * in_scale * scale)).astype(jnp.bfloat16)

    return at


def source_of(half, case):
    up = jnp.where(case == 1, 4, jnp.where(case == 2, 1, 3))
    down = jnp.where(case == 1, 2, jnp.where(case == 2, 3, 4))
    return jnp.where(case == 0, 0, jnp.where(half == 0, up, down))


def partner_at(half, case, near_up, near_down, *parts):
    chosen = source_of(half, case)

    def at(cols):
        partner = jnp.where(half == 0, near_up[:, cols], near_down[:, cols])
        for source, part in enumerate(parts, 1):
            partner = jnp.where(chosen == source, part[:, cols], partner)
        return partner

    return at


def renew_kernel(scale, up, down, slope_up, slope_down, grad, out_up, out_down):
    step_up = stepped(slope_up[...].T, grad, scale[0])
    step_down = stepped(slope_down[...].T, grad, scale[0])

    def body(cols):
        out_up[:, cols] = up[:, cols] - step_up(cols)
        out_down[:, cols] = down[:, cols] - step_down(cols)

    strips(grad.shape[1], body)


def renewed(scale, weights, slope, grad, begin, end):
    rows, columns = weights.shape
    depth, base = slope.shape[0], rows // (2 * BLOCK)
    first, blocks = begin // BLOCK, (end - begin) // BLOCK
    block = (BLOCK, columns)
    shape = jax.ShapeDtypeStruct((end - begin, columns), weights.dtype)
    size = (end - begin) * columns
    return pl.pallas_call(
        renew_kernel,
        grid=(blocks,),
        in_specs=[
            pl.BlockSpec(memory_space=pltpu.SMEM),
            pl.BlockSpec(block, lambda i: (first + i, 0)),
            pl.BlockSpec(block, lambda i: (base + first + i, 0)),
            pl.BlockSpec((depth, BLOCK), lambda i: (0, first + i)),
            pl.BlockSpec((depth, BLOCK), lambda i: (0, base + first + i)),
            pl.BlockSpec((depth, columns), lambda i: (0, 0)),
        ],
        out_specs=[pl.BlockSpec(block, lambda i: (i, 0))] * 2,
        out_shape=[shape] * 2,
        cost_estimate=pl.CostEstimate(
            flops=4 * size * depth, bytes_accessed=8 * size, transcendentals=0
        ),
        compiler_params=pltpu.CompilerParams(vmem_limit_bytes=24 << 20),
    )(scale, weights, weights, slope, slope, grad)


def average_kernel(case_ref, scales, weights, slope, slope_other, grad, grad_other, *rest):
    sources, out = rest[:6], rest[-1]
    mine = stepped(slope[...].T, grad, scales[0])
    theirs = stepped(slope_other[...].T, grad_other, scales[1])
    partner = partner_at(pl.program_id(0), case_ref[0], *sources)

    def body(cols):
        own = weights[:, cols] - mine(cols)
        out[:, cols] = (own + (partner(cols) - theirs(cols))) * 0.5

    strips(weights.shape[1], body)


def plain_kernel(begin, case_ref, *refs):
    new, near, (above, below, from_up, from_down) = refs[:2], refs[2:4], refs[4:8]
    out, own, part, sems = refs[-4:]
    rows, base = own.shape[1], out.shape[0] // 2
    kinds = (near, (from_down, below), (above, from_up), (from_up, from_down))

    def average(partner):
        loads = []
        for half in range(2):
            loads.append(pltpu.make_async_copy(new[half], own.at[half], sems.at[0, half]))
            loads.append(pltpu.make_async_copy(partner[half], part.at[half], sems.at[1, half]))
        for load in loads:
            load.start()
        stores = []
        for half in range(2):
            loads[2 * half].wait()
            loads[2 * half + 1].wait()

            def body(number, carry, half=half):
                at = pl.ds(pl.multiple_of(number * 64, 64), 64)
                own[half, at] = (own[half, at] + part[half, at]) * 0.5
                return carry

            lax.fori_loop(0, rows // 64, body, 0)
            place = out.at[pl.ds(half * base + begin, rows)]
            stores.append(pltpu.make_async_copy(own.at[half], place, sems.at[2, half]))
            stores[half].start()
        for store in stores:
            store.wait()

    for kind, partner in enumerate(kinds):

        @pl.when(case_ref[0] == kind)
        def _(partner=partner):
            average(partner)


def averaged(kernel, case, own, own_specs, sources, begin, end, shape, out):
    rows, columns = shape
    first, blocks = begin // BLOCK, (end - begin) // BLOCK
    base = rows // (2 * BLOCK)
    block = (BLOCK, columns)

    def near_map(wanted):
        def index(half, i, case_ref):
            used = (half == wanted) & (case_ref[0] == 0)
            return (jnp.where(used, i, 0), 0)

        return index

    def part_map(number):
        def index(half, i, case_ref):
            return (jnp.where(source_of(half, case_ref[0]) == number, i, 0), 0)

        return index

    in_specs = own_specs + [pl.BlockSpec(block, near_map(wanted)) for wanted in range(2)]
    in_specs += [pl.BlockSpec(block, part_map(number)) for number in range(1, 5)]
    operands = [case.reshape(1), *own, *sources]
    aliases = {}
    if out is not None:
        in_specs.append(pl.BlockSpec(memory_space=pl.ANY))
        aliases = {len(operands): 0}
        operands.append(out)
    size = 2 * blocks * BLOCK * columns
    return pl.pallas_call(
        kernel,
        grid_spec=pltpu.PrefetchScalarGridSpec(
            num_scalar_prefetch=1,
            grid=(2, blocks),
            in_specs=in_specs,
            out_specs=pl.BlockSpec(block, lambda half, i, case_ref: (half * base + first + i, 0)),
        ),
        out_shape=jax.ShapeDtypeStruct(shape, jnp.bfloat16),
        input_output_aliases=aliases,
        cost_estimate=pl.CostEstimate(flops=4 * size, bytes_accessed=6 * size, transcendentals=0),
        compiler_params=pltpu.CompilerParams(vmem_limit_bytes=40 << 20),
    )(*operands)


def averaged_weights(case, scales, weights, slopes, grads, sources, end, out):
    rows, columns = weights.shape
    depth, base, short = slopes[0].shape[0], rows // (2 * BLOCK), end // BLOCK
    fixed = pl.BlockSpec((depth, columns), lambda half, i, case_ref: (0, 0))
    own_specs = [
        pl.BlockSpec(memory_space=pltpu.SMEM),
        pl.BlockSpec((BLOCK, columns), lambda half, i, case_ref: (half * base + i, 0)),
        pl.BlockSpec((depth, BLOCK), lambda half, i, case_ref: (0, half * base + i)),
        pl.BlockSpec((depth, BLOCK), lambda half, i, case_ref: (0, half * short + i)),
        fixed,
        fixed,
    ]
    own = (scales, weights, *slopes, *grads)
    return averaged(average_kernel, case, own, own_specs, sources, 0, end, weights.shape, out)


def averaged_updates(case, own, sources, begin, end, shape, out):
    block = (2, end - begin, shape[1])
    anywhere = pl.BlockSpec(memory_space=pl.ANY)
    size = (end - begin) * shape[1]
    return pl.pallas_call(
        partial(plain_kernel, begin),
        in_specs=[pl.BlockSpec(memory_space=pltpu.SMEM)] + [anywhere] * 9,
        out_specs=anywhere,
        out_shape=jax.ShapeDtypeStruct(shape, jnp.bfloat16),
        input_output_aliases={9: 0},
        scratch_shapes=[
            pltpu.VMEM(block, jnp.bfloat16),
            pltpu.VMEM(block, jnp.bfloat16),
            pltpu.SemaphoreType.DMA((3, 2)),
        ],
        cost_estimate=pl.CostEstimate(flops=4 * size, bytes_accessed=12 * size, transcendentals=0),
        compiler_params=pltpu.CompilerParams(vmem_limit_bytes=24 << 20),
    )(case.reshape(1), *own, *sources, out)


def squares_kernel(slope, grad, key_grad, out, total):
    step = pl.program_id(0)

    @pl.when(step == 0)
    def _():
        total[...] = jnp.zeros_like(total)

    rows = slope[...].T
    columns = grad.shape[1]

    def added(grads):
        gradient = dot(rows, grads, ROWS_COLS)
        return jnp.sum((gradient * gradient).reshape(-1, 8, gradient.shape[1]), axis=0)

    def strip(number, carry):
        cols = pl.ds(pl.multiple_of(number * STRIP, STRIP), STRIP)
        total[...] += added(grad[:, cols])
        return carry

    lax.fori_loop(0, columns // STRIP, strip, 0)
    total[:, :HEAD] += added(key_grad[...]) * 0.5

    @pl.when(step == pl.num_programs(0) - 1)
    def _():
        out[...] = jnp.sum(total[...], keepdims=True)


def gradient_squares(slope, grad, key_grad):
    depth, rows = slope.shape
    in_scale = rows ** (-0.5)
    size = rows * (grad.shape[1] + HEAD) * depth
    block = rows // 3
    squares = pl.pallas_call(
        squares_kernel,
        grid=(rows // block,),
        in_specs=[
            pl.BlockSpec((depth, block), lambda i: (0, i)),
            pl.BlockSpec(grad.shape, lambda i: (0, 0)),
            pl.BlockSpec(key_grad.shape, lambda i: (0, 0)),
        ],
        out_specs=pl.BlockSpec((1, 1), lambda i: (0, 0)),
        out_shape=jax.ShapeDtypeStruct((1, 1), jnp.float32),
        scratch_shapes=[pltpu.VMEM((8, STRIP), jnp.float32)],
        cost_estimate=pl.CostEstimate(
            flops=2 * size, bytes_accessed=2 * slope.size + 2 * grad.size, transcendentals=0
        ),
        compiler_params=pltpu.CompilerParams(vmem_limit_bytes=16 << 20),
    )(slope, grad, key_grad)
    return squares[0, 0] * (in_scale * in_scale)


def source_of(half, case):
    up = jnp.where(case == 1, 4, jnp.where(case == 2, 1, 3))
    down = jnp.where(case == 1, 2, jnp.where(case == 2, 3, 4))
    return jnp.where(case == 0, 0, jnp.where(half == 0, up, down))


def settled_kernel(a_ref, b_ref, c_ref, d_ref):
    c_ref[...] = a_ref[...]
    d_ref[...] = b_ref[...]


def settled(a, b):
    block = pl.BlockSpec((64, a.shape[1]), lambda i: (i, 0))
    return pl.pallas_call(
        settled_kernel,
        grid=(a.shape[0] // 64,),
        in_specs=[block, block],
        out_specs=[block, block],
        out_shape=[jax.ShapeDtypeStruct(x.shape, x.dtype) for x in (a, b)],
        cost_estimate=pl.CostEstimate(flops=0, bytes_accessed=8 * a.size, transcendentals=0),
        compiler_params=pltpu.CompilerParams(vmem_limit_bytes=8 << 20),
    )(a, b)


def section(fwd_in, bwd_in, bwd_grad, seg_fwd, seg_bwd, w_query, w_key, gain, gossip_exp):
    query_weight = w_query[0, 0]
    key_weight = w_key[0, 0]
    gain_local = gain[0, 0]
    fwd_rows = fwd_in[0, 0]
    bwd_rows = bwd_in[0, 0]
    grad_rows = bwd_grad[0, 0]
    count, local_width = fwd_rows.shape
    pipe_count = lax.axis_size("pipe")
    tp_index = lax.axis_index("tp")
    low = tp_index == 0
    offset = tp_index * local_width
    gossip = Gossip(gossip_exp[0])

    width = query_weight.shape[0]
    in_scale = width ** (-0.5)
    half, early_rows = width // 2, width // 4
    cuts = ((early_rows, half - BLOCK), (half - BLOCK, half))
    parts = query_weight[:early_rows], query_weight[half : half + early_rows]
    sent = gossip.first(*parts)
    near = [flipped(part, "rep", 0) for part in parts]

    beside = jnp.broadcast_to(gain_local[None], (16, local_width))
    other = flipped(jnp.concatenate([bwd_rows, beside], axis=0), "tp", 0)
    bwd_full = in_order(bwd_rows, other[:count], low, 1)
    gain_full = in_order(gain_local, other[count], low, 0)

    _, scaled_b, inv_b, normed_b = normalize(bwd_full, gain_full)
    own_values_b = lax.dynamic_slice_in_dim(normed_b, offset, local_width, 1)
    key_rows = lax.dynamic_slice_in_dim(key_weight, offset, local_width, 0)
    early = gossip.small(own_values_b[:, :early_rows])
    early_other = flipped(early, "tp", 0)
    normed_partner = in_order(early, early_other, low, 1)

    queries = projected(normed_b, query_weight)
    keys = projected(normed_b, key_weight)
    query_grad, value_grad, key_part = per_head(
        back_kernel,
        seg_bwd[0, 0],
        queries,
        keys,
        (own_values_b, grad_rows),
        (
            ((count, local_width), jnp.bfloat16),
            ((count, local_width), jnp.float32),
            ((count, HEAD), jnp.bfloat16),
        ),
        5,
    )

    query_grad_partner = gossip.small(query_grad)
    key_other = flipped(key_part, "tp", 0)
    key_grad = (key_part.astype(jnp.float32) + key_other.astype(jnp.float32)).astype(jnp.bfloat16)

    contract_last = (((1,), (1,)), ((), ()))
    partial_grad = (
        lax.dot_general(query_grad, query_weight, contract_last, preferred_element_type=jnp.float32)
        * in_scale
    )
    own_part = (lax.dynamic_slice_in_dim(partial_grad, offset, local_width, 1) + value_grad).astype(
        jnp.bfloat16
    )
    other_part = lax.dynamic_slice_in_dim(
        partial_grad, local_width - offset, local_width, 1
    ).astype(jnp.bfloat16)
    from_other = flipped(other_part, "tp", 0)
    full_grad = (
        own_part.astype(jnp.float32)
        + from_other.astype(jnp.float32)
        + lax.dot_general(key_grad, key_rows, contract_last, preferred_element_type=jnp.float32)
        * in_scale
    )
    own_scaled = lax.dynamic_slice_in_dim(scaled_b, offset, local_width, 1)
    weighted = full_grad * gain_local.astype(jnp.float32)
    sums = jnp.stack([jnp.sum(weighted, axis=-1), jnp.sum(weighted * own_scaled, axis=-1)])
    means = (sums + flipped(sums, "tp", 0)) / width
    input_grad = inv_b * (weighted - means[0][:, None] - own_scaled * means[1][:, None])
    grad_gain = jnp.sum(full_grad * own_scaled, axis=0)
    back_rows = (grad_rows.astype(jnp.float32) + input_grad).astype(jnp.bfloat16)
    prev_rows = from_behind(back_rows, "pipe", -1)

    contract_first = (((0,), (0,)), ((), ()))

    def weight_grad(rows, grad):
        return (
            lax.dot_general(rows, grad, contract_first, preferred_element_type=jnp.float32)
            * in_scale
        )

    query_squares = gradient_squares(normed_b, query_grad, key_grad)
    grad_key = weight_grad(own_values_b, key_grad)
    local_squares = query_squares + jnp.sum(grad_gain * grad_gain)
    fwd_other = flipped(fwd_rows, "tp", 0)
    fwd_other, local_squares = lax.optimization_barrier((fwd_other, local_squares))
    fwd_full = in_order(fwd_rows, fwd_other, low, 1)
    _, _, _, normed = normalize(fwd_full, gain_full)
    own_values = lax.dynamic_slice_in_dim(normed, offset, local_width, 1)
    queries_f = projected(normed, query_weight)
    keys_f = projected(normed, key_weight)
    (section_out,) = per_head(
        onward_kernel,
        seg_fwd[0, 0],
        queries_f,
        keys_f,
        (own_values, fwd_rows),
        (((count, local_width), jnp.bfloat16),),
        2,
    )
    next_rows = from_behind(section_out, "pipe", 1)

    total_squares = of_everyone(local_squares, ("pipe", "tp"))
    total = pipe_count * (width * width + width * HEAD + width)
    inverse = lax.rsqrt(total_squares / total + STEP_EPS)

    def step_of(gradient, scale):
        return (LEARN_RATE * gradient * scale).astype(jnp.bfloat16)

    gain_new = updated(gain_local, step_of(grad_gain, inverse))
    both = gossip.tiny(
        jnp.concatenate([gain_new.astype(jnp.float32), jnp.broadcast_to(inverse, (HEAD,))])
    )
    gain_partner = both[:local_width].astype(jnp.bfloat16)
    inverse_partner = both[local_width]
    gain_out = halves(gain_new, gain_partner)

    key_new = updated(key_rows, step_of(grad_key, inverse))
    key_half = halves(key_new, gossip.small(key_new))
    key_out = in_order(key_half, flipped(key_half, "tp", 0), low, 0)

    news = []
    for begin, end in cuts:
        new = renewed(inverse.reshape(1), query_weight, normed_b, query_grad, begin, end)
        state = gossip.first(*new)
        new_near = [flipped(part, "rep", 0) for part in new]
        later = gossip.second(state)
        news.append((new, (*new_near, *later)))

    sources = (*near, *gossip.second(sent))
    next_rows, prev_rows = settled(next_rows, prev_rows)
    query_out = averaged_weights(
        gossip.case,
        jnp.stack([inverse, inverse_partner]),
        query_weight,
        (normed_b, normed_partner),
        (query_grad, query_grad_partner),
        sources,
        early_rows,
        None,
    )
    for number, (begin, end) in enumerate(cuts):
        query_out = averaged_updates(
            gossip.case, *news[number], begin, end, query_weight.shape, query_out
        )
    return (
        next_rows[None, None],
        prev_rows[None, None],
        query_out[None, None],
        key_out[None, None],
        gain_out[None, None],
    )


def solution(mesh):
    return jax.shard_map(
        section,
        mesh=mesh,
        in_specs=(
            P("rep", "pipe", None, "tp"),
            P("rep", "pipe", None, "tp"),
            P("rep", "pipe", None, "tp"),
            P("rep", "pipe", None),
            P("rep", "pipe", None),
            P("rep", "pipe", None, "tp"),
            P("rep", "pipe", None, None),
            P("rep", "pipe", "tp"),
            P("pipe"),
        ),
        out_specs=(
            P("rep", "pipe", None, "tp"),
            P("rep", "pipe", None, "tp"),
            P("rep", "pipe", None, "tp"),
            P("rep", "pipe", None, None),
            P("rep", "pipe", "tp"),
        ),
        check_vma=False,
    )
```

```python
from functools import partial

import jax
import jax.numpy as jnp
from jax import lax
from jax.experimental import pallas as pl
from jax.experimental.pallas import tpu as pltpu
from jax.sharding import PartitionSpec as P


HEAD = 128


LN_EPS = 1e-05
STEP_EPS = 1e-06
LEARN_RATE = 0.2
MASK_FILL = -1e30
BLOCK = 256
EDGE = 128
TOGETHER = 2
STRIP = 512


def from_behind(shard, axis, by):
    length = lax.axis_size(axis)
    return lax.ppermute(shard, axis, [(i, (i + by) % length) for i in range(length)])


def flipped(block, axis, bit):
    return lax.ppermute(block, axis, [(i, i ^ 1 << bit) for i in range(lax.axis_size(axis))])


def in_order(own, other, low, axis):
    return jnp.where(
        low, jnp.concatenate([own, other], axis), jnp.concatenate([other, own], axis)
    )


def of_everyone(shard, axis):
    copies = jnp.broadcast_to(shard, (lax.axis_size(axis), *shard.shape))
    return jnp.sum(lax.all_to_all(copies, axis, split_axis=0, concat_axis=0, tiled=True), axis=0)


def relay_kernel(case_ref, up, down, above_in, below_in, above, below, held, sem):
    def carry(source, target):
        for one, other in ((source, held), (held, target)):
            copy = pltpu.make_async_copy(one, other, sem)
            copy.start()
            copy.wait()

    @pl.when(case_ref[0] == 1)
    def _():
        carry(down, above)

    @pl.when(case_ref[0] == 2)
    def _():
        carry(up, below)


def relayed(case, up, down, above, below):
    anywhere = pl.BlockSpec(memory_space=pl.ANY)
    return pl.pallas_call(
        relay_kernel,
        in_specs=[pl.BlockSpec(memory_space=pltpu.SMEM)] + [anywhere] * 4,
        out_specs=[anywhere] * 2,
        out_shape=[jax.ShapeDtypeStruct(up.shape, up.dtype)] * 2,
        input_output_aliases={3: 0, 4: 1},
        scratch_shapes=[pltpu.VMEM(up.shape, up.dtype), pltpu.SemaphoreType.DMA],
        cost_estimate=pl.CostEstimate(flops=0, bytes_accessed=up.size, transcendentals=0),
        compiler_params=pltpu.CompilerParams(vmem_limit_bytes=8 << 20),
    )(case.reshape(1), up, down, above, below)


class Gossip:
    def __init__(self, exponent):
        self.exponent = exponent
        odd = (lax.axis_index("rep") // 2) % 2
        self.case = jnp.where(exponent == 2, 3, jnp.where(exponent == 1, 1 + odd, 0))

    def first(self, up, down):
        return up, down, from_behind(up, "rep", 2), from_behind(down, "rep", -2)

    def second(self, state):
        above, below = relayed(self.case, *state)
        return above, below, from_behind(above, "rep", 2), from_behind(below, "rep", -2)

    def small(self, block):
        half = block.shape[0] // 2
        up, down, block = lax.optimization_barrier((block[:half], block[half:], block))
        state = self.first(up, down)
        above, below, from_up, from_down = self.second(state)
        near = flipped(block, "rep", 0)
        case = self.case

        def pick(a, b, c, d):
            return jnp.where(case == 0, a, jnp.where(case == 1, b, jnp.where(case == 2, c, d)))

        return jnp.concatenate(
            [
                pick(near[:half], from_down, above, from_up),
                pick(near[half:], below, from_up, from_down),
            ],
            axis=0,
        )

    def tiny(self, block):
        results = [flipped(block, "rep", bit) for bit in range(3)]
        return jnp.where(
            self.exponent == 0, results[0], jnp.where(self.exponent == 1, results[1], results[2])
        )


def normalize(rows, gain_full):
    values = rows.astype(jnp.float32)
    centred = values - jnp.mean(values, axis=-1, keepdims=True)
    inv_std = lax.rsqrt(jnp.mean(centred * centred, axis=-1, keepdims=True) + LN_EPS)
    scaled = centred * inv_std
    normed = (scaled * gain_full.astype(jnp.float32)).astype(jnp.bfloat16)
    return (values, scaled, inv_std, normed)


def projected(normed, weight):
    in_scale = normed.shape[1] ** (-0.5)
    product = jnp.dot(normed, weight, preferred_element_type=jnp.float32)
    return (product * in_scale).astype(jnp.bfloat16)


def dot(a, b, over):
    return lax.dot_general(a, b, (over, ((), ())), preferred_element_type=jnp.float32)


ROWS_COLS, LAST_LAST, FIRST_FIRST = ((1,), (0,)), ((1,), (1,)), ((0,), (0,))


def head_probs(queries, keys, tall, wide):
    scores = dot(queries, keys, LAST_LAST) * HEAD ** (-0.5)
    scores = jnp.where(tall == wide, scores, MASK_FILL)
    peak = jnp.max(scores, axis=-1, keepdims=True)
    expo = jnp.exp(scores - peak)
    return (expo / jnp.sum(expo, axis=-1, keepdims=True)).astype(jnp.bfloat16)


def head_columns():
    return [slice(head * HEAD, (head + 1) * HEAD) for head in range(TOGETHER)]


def onward_kernel(queries, keys, values, rows, tall, wide, out):
    for cols in head_columns():
        probs = head_probs(queries[:, cols], keys[...], tall[...], wide[...])
        mixed = dot(probs, values[:, cols], ROWS_COLS)
        out[:, cols] = (rows[:, cols].astype(jnp.float32) + mixed).astype(jnp.bfloat16)


def back_kernel(queries, keys, values, grads, tall, wide, query_grad, value_grad, key_part, total):
    group = pl.program_id(0)

    @pl.when(group == 0)
    def _():
        total[...] = jnp.zeros_like(total)

    key, terms = keys[...], []
    for cols in head_columns():
        query, grad = queries[:, cols], grads[:, cols]
        probs = head_probs(query, key, tall[...], wide[...])
        prob_f = probs.astype(jnp.float32)
        value_grad[:, cols] = dot(probs, grad, FIRST_FIRST)
        prob_grad = dot(grad, values[:, cols], LAST_LAST)
        inner = jnp.sum(prob_grad * prob_f, axis=-1, keepdims=True)
        score_grad = (prob_f * (prob_grad - inner) * HEAD ** (-0.5)).astype(jnp.bfloat16)
        query_grad[:, cols] = dot(score_grad, key, ROWS_COLS).astype(jnp.bfloat16)
        terms.append(dot(score_grad, query, FIRST_FIRST))
    total[...] += sum(terms)

    @pl.when(group == pl.num_programs(0) - 1)
    def _():
        key_part[...] = total[...].astype(jnp.bfloat16)


def per_head(kernel, caption, queries, keys, extras, outs, products):
    count, width = queries.shape
    heads = width // HEAD
    by_head = pl.BlockSpec((count, TOGETHER * HEAD), lambda h: (0, h))
    fixed = pl.BlockSpec((count, HEAD), lambda h: (0, 0))
    specs = [by_head, fixed] + [by_head] * len(extras)
    specs += [pl.BlockSpec((count, 1), lambda h: (0, 0)), pl.BlockSpec((1, count), lambda h: (0, 0))]
    backward = len(outs) > 1
    return pl.pallas_call(
        kernel,
        grid=(heads // TOGETHER,),
        in_specs=specs,
        out_specs=[by_head if shape[1] == width else fixed for shape, kind in outs],
        out_shape=[jax.ShapeDtypeStruct(shape, kind) for shape, kind in outs],
        scratch_shapes=[pltpu.VMEM((count, HEAD), jnp.float32)] if backward else [],
        cost_estimate=pl.CostEstimate(
            flops=2 * products * heads * count * count * HEAD,
            bytes_accessed=2 * (len(extras) + 1 + len(outs)) * count * width,
            transcendentals=heads * count * count,
        ),
        compiler_params=pltpu.CompilerParams(vmem_limit_bytes=24 << 20),
    )(queries, keys, *extras, caption[:, None], caption[None, :])


def updated(weight, step):
    return (weight.astype(jnp.float32) - step.astype(jnp.float32)).astype(jnp.bfloat16)


def halves(mine, theirs):
    return ((mine.astype(jnp.float32) + theirs.astype(jnp.float32)) * 0.5).astype(jnp.bfloat16)


def strips(columns, body):
    def at(number, carry):
        body(pl.ds(pl.multiple_of(number * STRIP, STRIP), STRIP))
        return carry

    lax.fori_loop(0, columns // STRIP, at, 0)


def stepped(rows, grads, scale):
    in_scale = (2 * grads.shape[1]) ** (-0.5)

    def at(cols):
        gradient = dot(rows, grads[:, cols], ROWS_COLS)
        return (gradient * (LEARN_RATE * in_scale * scale)).astype(jnp.bfloat16)

    return at


def source_of(half, case):
    up = jnp.where(case == 1, 4, jnp.where(case == 2, 1, 3))
    down = jnp.where(case == 1, 2, jnp.where(case == 2, 3, 4))
    return jnp.where(case == 0, 0, jnp.where(half == 0, up, down))


def partner_at(half, case, near_up, near_down, *parts):
    chosen = source_of(half, case)

    def at(cols):
        partner = jnp.where(half == 0, near_up[:, cols], near_down[:, cols])
        for source, part in enumerate(parts, 1):
            partner = jnp.where(chosen == source, part[:, cols], partner)
        return partner

    return at


def cut_kernel(weights, up, down, held, sems):
    rows, base = up.shape[0], weights.shape[0] // 2
    pieces = [
        (half, pl.ds(half * base + start, BLOCK), pl.ds(start, BLOCK))
        for start in range(0, rows, BLOCK)
        for half in range(2)
    ]
    loads = [
        pltpu.make_async_copy(weights.at[there], held.at[half, here], sems.at[0, number])
        for number, (half, there, here) in enumerate(pieces)
    ]
    stores = [
        pltpu.make_async_copy(held.at[half, here], (up, down)[half].at[here], sems.at[1, number])
        for number, (half, there, here) in enumerate(pieces)
    ]
    for load in loads:
        load.start()
    for load, store in zip(loads, stores):
        load.wait()
        store.start()
    for store in stores:
        store.wait()


def cut_out(weights, rows):
    columns = weights.shape[1]
    anywhere = pl.BlockSpec(memory_space=pl.ANY)
    return pl.pallas_call(
        cut_kernel,
        in_specs=[anywhere],
        out_specs=[anywhere] * 2,
        out_shape=[jax.ShapeDtypeStruct((rows, columns), weights.dtype)] * 2,
        scratch_shapes=[
            pltpu.VMEM((2, rows, columns), weights.dtype),
            pltpu.SemaphoreType.DMA((2, 2 * rows // BLOCK)),
        ],
        cost_estimate=pl.CostEstimate(
            flops=0, bytes_accessed=8 * rows * columns, transcendentals=0
        ),
        compiler_params=pltpu.CompilerParams(vmem_limit_bytes=56 << 20),
    )(weights)


def renew_kernel(scale, up, down, slope_up, slope_down, grad, out_up, out_down):
    step_up = stepped(slope_up[...].T, grad, scale[0])
    step_down = stepped(slope_down[...].T, grad, scale[0])

    def body(cols):
        out_up[:, cols] = up[:, cols] - step_up(cols)
        out_down[:, cols] = down[:, cols] - step_down(cols)

    strips(grad.shape[1], body)


def renewed(scale, weights, slope, grad, begin, end):
    rows, columns = weights.shape
    depth, base = slope.shape[0], rows // (2 * EDGE)
    first, blocks = begin // EDGE, (end - begin) // EDGE
    block = (EDGE, columns)
    shape = jax.ShapeDtypeStruct((end - begin, columns), weights.dtype)
    size = (end - begin) * columns
    return pl.pallas_call(
        renew_kernel,
        grid=(blocks,),
        in_specs=[
            pl.BlockSpec(memory_space=pltpu.SMEM),
            pl.BlockSpec(block, lambda i: (first + i, 0)),
            pl.BlockSpec(block, lambda i: (base + first + i, 0)),
            pl.BlockSpec((depth, EDGE), lambda i: (0, first + i)),
            pl.BlockSpec((depth, EDGE), lambda i: (0, base + first + i)),
            pl.BlockSpec((depth, columns), lambda i: (0, 0)),
        ],
        out_specs=[pl.BlockSpec(block, lambda i: (i, 0))] * 2,
        out_shape=[shape] * 2,
        cost_estimate=pl.CostEstimate(
            flops=4 * size * depth, bytes_accessed=8 * size, transcendentals=0
        ),
        compiler_params=pltpu.CompilerParams(vmem_limit_bytes=56 << 20),
    )(scale, weights, weights, slope, slope, grad)


def average_kernel(case_ref, scales, weights, slope, slope_other, grad, grad_other, *rest):
    sources, out = rest[:6], rest[-1]
    mine = stepped(slope[...].T, grad, scales[0])
    theirs = stepped(slope_other[...].T, grad_other, scales[1])
    partner = partner_at(pl.program_id(0), case_ref[0], *sources)

    def body(cols):
        own = weights[:, cols] - mine(cols)
        out[:, cols] = (own + (partner(cols) - theirs(cols))) * 0.5

    strips(weights.shape[1], body)


def plain_kernel(begin, case_ref, *refs):
    new, near, (above, below, from_up, from_down) = refs[:2], refs[2:4], refs[4:8]
    out, own, part, sems = refs[-4:]
    rows, base = own.shape[1], out.shape[0] // 2
    kinds = (near, (from_down, below), (above, from_up), (from_up, from_down))

    def average(partner):
        loads = []
        for half in range(2):
            loads.append(pltpu.make_async_copy(new[half], own.at[half], sems.at[0, half]))
            loads.append(pltpu.make_async_copy(partner[half], part.at[half], sems.at[1, half]))
        for load in loads:
            load.start()
        stores = []
        for half in range(2):
            loads[2 * half].wait()
            loads[2 * half + 1].wait()

            def body(number, carry, half=half):
                at = pl.ds(pl.multiple_of(number * 64, 64), 64)
                own[half, at] = (own[half, at] + part[half, at]) * 0.5
                return carry

            lax.fori_loop(0, rows // 64, body, 0)
            place = out.at[pl.ds(half * base + begin, rows)]
            stores.append(pltpu.make_async_copy(own.at[half], place, sems.at[2, half]))
            stores[half].start()
        for store in stores:
            store.wait()

    for kind, partner in enumerate(kinds):

        @pl.when(case_ref[0] == kind)
        def _(partner=partner):
            average(partner)


def averaged(kernel, case, own, own_specs, sources, begin, end, shape, out):
    rows, columns = shape
    first, blocks = begin // BLOCK, (end - begin) // BLOCK
    base = rows // (2 * BLOCK)
    block = (BLOCK, columns)

    def near_map(wanted):
        def index(half, i, case_ref):
            used = (half == wanted) & (case_ref[0] == 0)
            return (jnp.where(used, i, 0), 0)

        return index

    def part_map(number):
        def index(half, i, case_ref):
            return (jnp.where(source_of(half, case_ref[0]) == number, i, 0), 0)

        return index

    in_specs = own_specs + [pl.BlockSpec(block, near_map(wanted)) for wanted in range(2)]
    in_specs += [pl.BlockSpec(block, part_map(number)) for number in range(1, 5)]
    operands = [case.reshape(1), *own, *sources]
    aliases = {}
    if out is not None:
        in_specs.append(pl.BlockSpec(memory_space=pl.ANY))
        aliases = {len(operands): 0}
        operands.append(out)
    size = 2 * blocks * BLOCK * columns
    return pl.pallas_call(
        kernel,
        grid_spec=pltpu.PrefetchScalarGridSpec(
            num_scalar_prefetch=1,
            grid=(2, blocks),
            in_specs=in_specs,
            out_specs=pl.BlockSpec(block, lambda half, i, case_ref: (half * base + first + i, 0)),
        ),
        out_shape=jax.ShapeDtypeStruct(shape, jnp.bfloat16),
        input_output_aliases=aliases,
        cost_estimate=pl.CostEstimate(flops=4 * size, bytes_accessed=6 * size, transcendentals=0),
        compiler_params=pltpu.CompilerParams(vmem_limit_bytes=40 << 20),
    )(*operands)


def averaged_weights(case, scales, weights, slopes, grads, sources, end, out):
    rows, columns = weights.shape
    depth, base, short = slopes[0].shape[0], rows // (2 * BLOCK), end // BLOCK
    fixed = pl.BlockSpec((depth, columns), lambda half, i, case_ref: (0, 0))
    own_specs = [
        pl.BlockSpec(memory_space=pltpu.SMEM),
        pl.BlockSpec((BLOCK, columns), lambda half, i, case_ref: (half * base + i, 0)),
        pl.BlockSpec((depth, BLOCK), lambda half, i, case_ref: (0, half * base + i)),
        pl.BlockSpec((depth, BLOCK), lambda half, i, case_ref: (0, half * short + i)),
        fixed,
        fixed,
    ]
    own = (scales, weights, *slopes, *grads)
    return averaged(average_kernel, case, own, own_specs, sources, 0, end, weights.shape, out)


def averaged_updates(case, own, sources, begin, end, shape, out):
    block = (2, end - begin, shape[1])
    anywhere = pl.BlockSpec(memory_space=pl.ANY)
    size = (end - begin) * shape[1]
    return pl.pallas_call(
        partial(plain_kernel, begin),
        in_specs=[pl.BlockSpec(memory_space=pltpu.SMEM)] + [anywhere] * 9,
        out_specs=anywhere,
        out_shape=jax.ShapeDtypeStruct(shape, jnp.bfloat16),
        input_output_aliases={9: 0},
        scratch_shapes=[
            pltpu.VMEM(block, jnp.bfloat16),
            pltpu.VMEM(block, jnp.bfloat16),
            pltpu.SemaphoreType.DMA((3, 2)),
        ],
        cost_estimate=pl.CostEstimate(flops=4 * size, bytes_accessed=12 * size, transcendentals=0),
        compiler_params=pltpu.CompilerParams(vmem_limit_bytes=24 << 20),
    )(case.reshape(1), *own, *sources, out)


def squares_kernel(slope, grad, key_grad, out, total):
    step = pl.program_id(0)

    @pl.when(step == 0)
    def _():
        total[...] = jnp.zeros_like(total)

    rows = slope[...].T
    columns = grad.shape[1]

    def added(grads):
        gradient = dot(rows, grads, ROWS_COLS)
        return jnp.sum((gradient * gradient).reshape(-1, 8, gradient.shape[1]), axis=0)

    def strip(number, carry):
        cols = pl.ds(pl.multiple_of(number * STRIP, STRIP), STRIP)
        total[...] += added(grad[:, cols])
        return carry

    lax.fori_loop(0, columns // STRIP, strip, 0)
    total[:, :HEAD] += added(key_grad[...]) * 0.5

    @pl.when(step == pl.num_programs(0) - 1)
    def _():
        out[...] = jnp.sum(total[...], keepdims=True)


def gradient_squares(slope, grad, key_grad):
    depth, rows = slope.shape
    in_scale = rows ** (-0.5)
    size = rows * (grad.shape[1] + HEAD) * depth
    block = rows // 3
    squares = pl.pallas_call(
        squares_kernel,
        grid=(rows // block,),
        in_specs=[
            pl.BlockSpec((depth, block), lambda i: (0, i)),
            pl.BlockSpec(grad.shape, lambda i: (0, 0)),
            pl.BlockSpec(key_grad.shape, lambda i: (0, 0)),
        ],
        out_specs=pl.BlockSpec((1, 1), lambda i: (0, 0)),
        out_shape=jax.ShapeDtypeStruct((1, 1), jnp.float32),
        scratch_shapes=[pltpu.VMEM((8, STRIP), jnp.float32)],
        cost_estimate=pl.CostEstimate(
            flops=2 * size, bytes_accessed=2 * slope.size + 2 * grad.size, transcendentals=0
        ),
        compiler_params=pltpu.CompilerParams(vmem_limit_bytes=16 << 20),
    )(slope, grad, key_grad)
    return squares[0, 0] * (in_scale * in_scale)


def source_of(half, case):
    up = jnp.where(case == 1, 4, jnp.where(case == 2, 1, 3))
    down = jnp.where(case == 1, 2, jnp.where(case == 2, 3, 4))
    return jnp.where(case == 0, 0, jnp.where(half == 0, up, down))


def settled_kernel(a_ref, b_ref, c_ref, d_ref):
    c_ref[...] = a_ref[...]
    d_ref[...] = b_ref[...]


def settled(a, b):
    block = pl.BlockSpec((64, a.shape[1]), lambda i: (i, 0))
    return pl.pallas_call(
        settled_kernel,
        grid=(a.shape[0] // 64,),
        in_specs=[block, block],
        out_specs=[block, block],
        out_shape=[jax.ShapeDtypeStruct(x.shape, x.dtype) for x in (a, b)],
        cost_estimate=pl.CostEstimate(flops=0, bytes_accessed=8 * a.size, transcendentals=0),
        compiler_params=pltpu.CompilerParams(vmem_limit_bytes=8 << 20),
    )(a, b)


def section(fwd_in, bwd_in, bwd_grad, seg_fwd, seg_bwd, w_query, w_key, gain, gossip_exp):
    query_weight = w_query[0, 0]
    key_weight = w_key[0, 0]
    gain_local = gain[0, 0]
    fwd_rows = fwd_in[0, 0]
    bwd_rows = bwd_in[0, 0]
    grad_rows = bwd_grad[0, 0]
    count, local_width = fwd_rows.shape
    pipe_count = lax.axis_size("pipe")
    tp_index = lax.axis_index("tp")
    low = tp_index == 0
    offset = tp_index * local_width
    gossip = Gossip(gossip_exp[0])

    width = query_weight.shape[0]
    in_scale = width ** (-0.5)
    half, early_rows = width // 2, width // 4
    cuts = ((early_rows, half - EDGE), (half - EDGE, half))
    parts = cut_out(query_weight, early_rows)
    sent = gossip.first(*parts)
    near = [flipped(part, "rep", 0) for part in parts]

    beside = jnp.broadcast_to(gain_local[None], (16, local_width))
    other = flipped(jnp.concatenate([bwd_rows, beside], axis=0), "tp", 0)
    bwd_full = in_order(bwd_rows, other[:count], low, 1)
    gain_full = in_order(gain_local, other[count], low, 0)

    _, scaled_b, inv_b, normed_b = normalize(bwd_full, gain_full)
    own_values_b = lax.dynamic_slice_in_dim(normed_b, offset, local_width, 1)
    key_rows = lax.dynamic_slice_in_dim(key_weight, offset, local_width, 0)
    early = gossip.small(own_values_b[:, :early_rows])
    early_other = flipped(early, "tp", 0)
    normed_partner = in_order(early, early_other, low, 1)

    queries = projected(normed_b, query_weight)
    keys = projected(normed_b, key_weight)
    query_grad, value_grad, key_part = per_head(
        back_kernel,
        seg_bwd[0, 0],
        queries,
        keys,
        (own_values_b, grad_rows),
        (
            ((count, local_width), jnp.bfloat16),
            ((count, local_width), jnp.float32),
            ((count, HEAD), jnp.bfloat16),
        ),
        5,
    )

    query_grad_partner = gossip.small(query_grad)
    key_other = flipped(key_part, "tp", 0)
    key_grad = (key_part.astype(jnp.float32) + key_other.astype(jnp.float32)).astype(jnp.bfloat16)

    contract_last = (((1,), (1,)), ((), ()))
    partial_grad = (
        lax.dot_general(query_grad, query_weight, contract_last, preferred_element_type=jnp.float32)
        * in_scale
    )
    own_part = (lax.dynamic_slice_in_dim(partial_grad, offset, local_width, 1) + value_grad).astype(
        jnp.bfloat16
    )
    other_part = lax.dynamic_slice_in_dim(
        partial_grad, local_width - offset, local_width, 1
    ).astype(jnp.bfloat16)
    from_other = flipped(other_part, "tp", 0)
    full_grad = (
        own_part.astype(jnp.float32)
        + from_other.astype(jnp.float32)
        + lax.dot_general(key_grad, key_rows, contract_last, preferred_element_type=jnp.float32)
        * in_scale
    )
    own_scaled = lax.dynamic_slice_in_dim(scaled_b, offset, local_width, 1)
    weighted = full_grad * gain_local.astype(jnp.float32)
    sums = jnp.stack([jnp.sum(weighted, axis=-1), jnp.sum(weighted * own_scaled, axis=-1)])
    means = (sums + flipped(sums, "tp", 0)) / width
    input_grad = inv_b * (weighted - means[0][:, None] - own_scaled * means[1][:, None])
    grad_gain = jnp.sum(full_grad * own_scaled, axis=0)
    back_rows = (grad_rows.astype(jnp.float32) + input_grad).astype(jnp.bfloat16)
    prev_rows = from_behind(back_rows, "pipe", -1)

    contract_first = (((0,), (0,)), ((), ()))

    def weight_grad(rows, grad):
        return (
            lax.dot_general(rows, grad, contract_first, preferred_element_type=jnp.float32)
            * in_scale
        )

    query_squares = gradient_squares(normed_b, query_grad, key_grad)
    grad_key = weight_grad(own_values_b, key_grad)
    local_squares = query_squares + jnp.sum(grad_gain * grad_gain)
    fwd_other = flipped(fwd_rows, "tp", 0)
    fwd_other, _ = lax.optimization_barrier((fwd_other, local_squares))
    fwd_full = in_order(fwd_rows, fwd_other, low, 1)
    _, _, _, normed = normalize(fwd_full, gain_full)
    own_values = lax.dynamic_slice_in_dim(normed, offset, local_width, 1)
    queries_f = projected(normed, query_weight)
    keys_f = projected(normed, key_weight)
    (section_out,) = per_head(
        onward_kernel,
        seg_fwd[0, 0],
        queries_f,
        keys_f,
        (own_values, fwd_rows),
        (((count, local_width), jnp.bfloat16),),
        2,
    )
    next_rows = from_behind(section_out, "pipe", 1)

    total_squares = of_everyone(local_squares, ("pipe", "tp"))
    total = pipe_count * (width * width + width * HEAD + width)
    inverse = lax.rsqrt(total_squares / total + STEP_EPS)

    def step_of(gradient, scale):
        return (LEARN_RATE * gradient * scale).astype(jnp.bfloat16)

    gain_new = updated(gain_local, step_of(grad_gain, inverse))
    both = gossip.tiny(
        jnp.concatenate([gain_new.astype(jnp.float32), jnp.broadcast_to(inverse, (HEAD,))])
    )
    gain_partner = both[:local_width].astype(jnp.bfloat16)
    inverse_partner = both[local_width]
    gain_out = halves(gain_new, gain_partner)

    key_new = updated(key_rows, step_of(grad_key, inverse))
    key_half = halves(key_new, gossip.small(key_new))
    key_out = in_order(key_half, flipped(key_half, "tp", 0), low, 0)

    news = []
    for begin, end in cuts:
        new = renewed(inverse.reshape(1), query_weight, normed_b, query_grad, begin, end)
        state = gossip.first(*new)
        new_near = [flipped(part, "rep", 0) for part in new]
        later = gossip.second(state)
        news.append((new, (*new_near, *later)))

    sources = (*near, *gossip.second(sent))
    next_rows, prev_rows = settled(next_rows, prev_rows)
    query_out = averaged_weights(
        gossip.case,
        jnp.stack([inverse, inverse_partner]),
        query_weight,
        (normed_b, normed_partner),
        (query_grad, query_grad_partner),
        sources,
        early_rows,
        None,
    )
    for number, (begin, end) in enumerate(cuts):
        query_out = averaged_updates(
            gossip.case, *news[number], begin, end, query_weight.shape, query_out
        )
    return (
        next_rows[None, None],
        prev_rows[None, None],
        query_out[None, None],
        key_out[None, None],
        gain_out[None, None],
    )


def solution(mesh):
    return jax.shard_map(
        section,
        mesh=mesh,
        in_specs=(
            P("rep", "pipe", None, "tp"),
            P("rep", "pipe", None, "tp"),
            P("rep", "pipe", None, "tp"),
            P("rep", "pipe", None),
            P("rep", "pipe", None),
            P("rep", "pipe", None, "tp"),
            P("rep", "pipe", None, None),
            P("rep", "pipe", "tp"),
            P("pipe"),
        ),
        out_specs=(
            P("rep", "pipe", None, "tp"),
            P("rep", "pipe", None, "tp"),
            P("rep", "pipe", None, "tp"),
            P("rep", "pipe", None, None),
            P("rep", "pipe", "tp"),
        ),
        check_vma=False,
    )
```

```python
from functools import partial

import jax
import jax.numpy as jnp
from jax import lax
from jax.experimental import pallas as pl
from jax.experimental.pallas import tpu as pltpu
from jax.sharding import PartitionSpec as P


HEAD = 128


LN_EPS = 1e-05
STEP_EPS = 1e-06
LEARN_RATE = 0.2
MASK_FILL = -1e30
BLOCK = 256
EDGE = 128
STRIP = 256


def from_behind(shard, axis, by):
    length = lax.axis_size(axis)
    return lax.ppermute(shard, axis, [(i, (i + by) % length) for i in range(length)])


def flipped(block, axis, bit):
    return lax.ppermute(block, axis, [(i, i ^ 1 << bit) for i in range(lax.axis_size(axis))])


def in_order(own, other, low, axis):
    return jnp.where(
        low, jnp.concatenate([own, other], axis), jnp.concatenate([other, own], axis)
    )


def of_everyone(shard, axis):
    copies = jnp.broadcast_to(shard, (lax.axis_size(axis), *shard.shape))
    return jnp.sum(lax.all_to_all(copies, axis, split_axis=0, concat_axis=0, tiled=True), axis=0)


def relay_kernel(case_ref, up, down, above_in, below_in, above, below, held, sem):
    def carry(source, target):
        for one, other in ((source, held), (held, target)):
            copy = pltpu.make_async_copy(one, other, sem)
            copy.start()
            copy.wait()

    @pl.when(case_ref[0] == 1)
    def _():
        carry(down, above)

    @pl.when(case_ref[0] == 2)
    def _():
        carry(up, below)


def relayed(case, up, down, above, below):
    anywhere = pl.BlockSpec(memory_space=pl.ANY)
    return pl.pallas_call(
        relay_kernel,
        in_specs=[pl.BlockSpec(memory_space=pltpu.SMEM)] + [anywhere] * 4,
        out_specs=[anywhere] * 2,
        out_shape=[jax.ShapeDtypeStruct(up.shape, up.dtype)] * 2,
        input_output_aliases={3: 0, 4: 1},
        scratch_shapes=[pltpu.VMEM(up.shape, up.dtype), pltpu.SemaphoreType.DMA],
        cost_estimate=pl.CostEstimate(flops=0, bytes_accessed=up.size, transcendentals=0),
        compiler_params=pltpu.CompilerParams(vmem_limit_bytes=8 << 20),
    )(case.reshape(1), up, down, above, below)


class Gossip:
    def __init__(self, exponent):
        self.exponent = exponent
        odd = (lax.axis_index("rep") // 2) % 2
        self.case = jnp.where(exponent == 2, 3, jnp.where(exponent == 1, 1 + odd, 0))

    def first(self, up, down):
        return up, down, from_behind(up, "rep", 2), from_behind(down, "rep", -2)

    def second(self, state):
        above, below = relayed(self.case, *state)
        return above, below, from_behind(above, "rep", 2), from_behind(below, "rep", -2)

    def small(self, block):
        half = block.shape[0] // 2
        up, down, block = lax.optimization_barrier((block[:half], block[half:], block))
        state = self.first(up, down)
        above, below, from_up, from_down = self.second(state)
        near = flipped(block, "rep", 0)
        case = self.case

        def pick(a, b, c, d):
            return jnp.where(case == 0, a, jnp.where(case == 1, b, jnp.where(case == 2, c, d)))

        return jnp.concatenate(
            [
                pick(near[:half], from_down, above, from_up),
                pick(near[half:], below, from_up, from_down),
            ],
            axis=0,
        )

    def tiny(self, block):
        results = [flipped(block, "rep", bit) for bit in range(3)]
        return jnp.where(
            self.exponent == 0, results[0], jnp.where(self.exponent == 1, results[1], results[2])
        )


def normalize(rows, gain_full):
    values = rows.astype(jnp.float32)
    centred = values - jnp.mean(values, axis=-1, keepdims=True)
    inv_std = lax.rsqrt(jnp.mean(centred * centred, axis=-1, keepdims=True) + LN_EPS)
    scaled = centred * inv_std
    normed = (scaled * gain_full.astype(jnp.float32)).astype(jnp.bfloat16)
    return (values, scaled, inv_std, normed)


def projected(normed, weight):
    in_scale = normed.shape[1] ** (-0.5)
    product = jnp.dot(normed, weight, preferred_element_type=jnp.float32)
    return (product * in_scale).astype(jnp.bfloat16)


def dot(a, b, over):
    return lax.dot_general(a, b, (over, ((), ())), preferred_element_type=jnp.float32)


ROWS_COLS, LAST_LAST, FIRST_FIRST = ((1,), (0,)), ((1,), (1,)), ((0,), (0,))


def head_probs(queries, keys, tall, wide):
    scores = dot(queries, keys, LAST_LAST) * HEAD ** (-0.5)
    scores = jnp.where(tall == wide, scores, MASK_FILL)
    peak = jnp.max(scores, axis=-1, keepdims=True)
    expo = jnp.exp(scores - peak)
    return (expo / jnp.sum(expo, axis=-1, keepdims=True)).astype(jnp.bfloat16)


def head_columns(ref):
    return [slice(begin, begin + HEAD) for begin in range(0, ref.shape[1], HEAD)]


def onward_kernel(queries, keys, values, rows, tall, wide, out):
    for cols in head_columns(queries):
        probs = head_probs(queries[:, cols], keys[...], tall[...], wide[...])
        mixed = dot(probs, values[:, cols], ROWS_COLS)
        out[:, cols] = (rows[:, cols].astype(jnp.float32) + mixed).astype(jnp.bfloat16)


def back_kernel(queries, keys, values, grads, tall, wide, query_grad, value_grad, key_part, total):
    group = pl.program_id(0)

    @pl.when(group == 0)
    def _():
        total[...] = jnp.zeros_like(total)

    key, terms = keys[...], []
    for cols in head_columns(queries):
        query, grad = queries[:, cols], grads[:, cols]
        probs = head_probs(query, key, tall[...], wide[...])
        prob_f = probs.astype(jnp.float32)
        value_grad[:, cols] = dot(probs, grad, FIRST_FIRST)
        prob_grad = dot(grad, values[:, cols], LAST_LAST)
        inner = jnp.sum(prob_grad * prob_f, axis=-1, keepdims=True)
        score_grad = (prob_f * (prob_grad - inner) * HEAD ** (-0.5)).astype(jnp.bfloat16)
        query_grad[:, cols] = dot(score_grad, key, ROWS_COLS).astype(jnp.bfloat16)
        terms.append(dot(score_grad, query, FIRST_FIRST))
    total[...] += sum(terms)

    @pl.when(group == pl.num_programs(0) - 1)
    def _():
        key_part[...] = total[...].astype(jnp.bfloat16)


def per_head(kernel, caption, queries, keys, extras, outs, products):
    count, width = queries.shape
    heads = width // HEAD
    backward = len(outs) > 1
    together = 2 if backward else 1
    by_head = pl.BlockSpec((count, together * HEAD), lambda h: (0, h))
    fixed = pl.BlockSpec((count, HEAD), lambda h: (0, 0))
    specs = [by_head, fixed] + [by_head] * len(extras)
    specs += [pl.BlockSpec((count, 1), lambda h: (0, 0)), pl.BlockSpec((1, count), lambda h: (0, 0))]
    return pl.pallas_call(
        kernel,
        grid=(heads // together,),
        in_specs=specs,
        out_specs=[by_head if shape[1] == width else fixed for shape, kind in outs],
        out_shape=[jax.ShapeDtypeStruct(shape, kind) for shape, kind in outs],
        scratch_shapes=[pltpu.VMEM((count, HEAD), jnp.float32)] if backward else [],
        cost_estimate=pl.CostEstimate(
            flops=2 * products * heads * count * count * HEAD,
            bytes_accessed=2 * (len(extras) + 1 + len(outs)) * count * width,
            transcendentals=heads * count * count,
        ),
        compiler_params=pltpu.CompilerParams(vmem_limit_bytes=24 << 20),
    )(queries, keys, *extras, caption[:, None], caption[None, :])


def updated(weight, step):
    return (weight.astype(jnp.float32) - step.astype(jnp.float32)).astype(jnp.bfloat16)


def halves(mine, theirs):
    return ((mine.astype(jnp.float32) + theirs.astype(jnp.float32)) * 0.5).astype(jnp.bfloat16)


def strips(columns, body):
    def at(number, carry):
        body(pl.ds(pl.multiple_of(number * STRIP, STRIP), STRIP))
        return carry

    lax.fori_loop(0, columns // STRIP, at, 0)


def stepped(rows, grads, scale):
    in_scale = (2 * grads.shape[1]) ** (-0.5)

    def at(cols):
        gradient = dot(rows, grads[:, cols], ROWS_COLS)
        return (gradient * (LEARN_RATE * in_scale * scale)).astype(jnp.bfloat16)

    return at


def source_of(half, case):
    up = jnp.where(case == 1, 4, jnp.where(case == 2, 1, 3))
    down = jnp.where(case == 1, 2, jnp.where(case == 2, 3, 4))
    return jnp.where(case == 0, 0, jnp.where(half == 0, up, down))


def partner_at(half, case, near_up, near_down, *parts):
    chosen = source_of(half, case)

    def at(cols):
        partner = jnp.where(half == 0, near_up[:, cols], near_down[:, cols])
        for source, part in enumerate(parts, 1):
            partner = jnp.where(chosen == source, part[:, cols], partner)
        return partner

    return at


def cut_kernel(begin, weights, up, down, held, sems):
    rows, base = up.shape[0], weights.shape[0] // 2
    pieces = [
        (half, pl.ds(half * base + begin + start, BLOCK), pl.ds(start, BLOCK))
        for start in range(0, rows, BLOCK)
        for half in range(2)
    ]
    loads = [
        pltpu.make_async_copy(weights.at[there], held.at[half, here], sems.at[0, number])
        for number, (half, there, here) in enumerate(pieces)
    ]
    stores = [
        pltpu.make_async_copy(held.at[half, here], (up, down)[half].at[here], sems.at[1, number])
        for number, (half, there, here) in enumerate(pieces)
    ]
    for load in loads:
        load.start()
    for load, store in zip(loads, stores):
        load.wait()
        store.start()
    for store in stores:
        store.wait()


def cut_out(weights, begin, end):
    rows, columns = end - begin, weights.shape[1]
    anywhere = pl.BlockSpec(memory_space=pl.ANY)
    return pl.pallas_call(
        partial(cut_kernel, begin),
        in_specs=[anywhere],
        out_specs=[anywhere] * 2,
        out_shape=[jax.ShapeDtypeStruct((rows, columns), weights.dtype)] * 2,
        scratch_shapes=[
            pltpu.VMEM((2, rows, columns), weights.dtype),
            pltpu.SemaphoreType.DMA((2, 2 * rows // BLOCK)),
        ],
        cost_estimate=pl.CostEstimate(
            flops=0, bytes_accessed=8 * rows * columns, transcendentals=0
        ),
        compiler_params=pltpu.CompilerParams(vmem_limit_bytes=56 << 20),
    )(weights)


def renew_kernel(scale, up, down, slope_up, slope_down, grad, out_up, out_down):
    step_up = stepped(slope_up[...].T, grad, scale[0])
    step_down = stepped(slope_down[...].T, grad, scale[0])

    def body(cols):
        out_up[:, cols] = up[:, cols] - step_up(cols)
        out_down[:, cols] = down[:, cols] - step_down(cols)

    strips(grad.shape[1], body)


def renewed(scale, weights, slope, grad, begin, end):
    rows, columns = weights.shape
    depth, base = slope.shape[0], rows // (2 * EDGE)
    first, blocks = begin // EDGE, (end - begin) // EDGE
    block = (EDGE, columns)
    shape = jax.ShapeDtypeStruct((end - begin, columns), weights.dtype)
    size = (end - begin) * columns
    return pl.pallas_call(
        renew_kernel,
        grid=(blocks,),
        in_specs=[
            pl.BlockSpec(memory_space=pltpu.SMEM),
            pl.BlockSpec(block, lambda i: (first + i, 0)),
            pl.BlockSpec(block, lambda i: (base + first + i, 0)),
            pl.BlockSpec((depth, EDGE), lambda i: (0, first + i)),
            pl.BlockSpec((depth, EDGE), lambda i: (0, base + first + i)),
            pl.BlockSpec((depth, columns), lambda i: (0, 0)),
        ],
        out_specs=[pl.BlockSpec(block, lambda i: (i, 0))] * 2,
        out_shape=[shape] * 2,
        cost_estimate=pl.CostEstimate(
            flops=4 * size * depth, bytes_accessed=8 * size, transcendentals=0
        ),
        compiler_params=pltpu.CompilerParams(vmem_limit_bytes=56 << 20),
    )(scale, weights, weights, slope, slope, grad)


def average_kernel(case_ref, scales, weights, slope, slope_other, grad, grad_other, *rest):
    sources, out = rest[:6], rest[-1]
    mine = stepped(slope[...].T, grad, scales[0])
    theirs = stepped(slope_other[...].T, grad_other, scales[1])
    partner = partner_at(pl.program_id(0), case_ref[0], *sources)

    def body(cols):
        own = weights[:, cols] - mine(cols)
        out[:, cols] = (own + (partner(cols) - theirs(cols))) * 0.5

    strips(weights.shape[1], body)


def plain_kernel(begin, case_ref, *refs):
    new, near, (above, below, from_up, from_down) = refs[:2], refs[2:4], refs[4:8]
    out, own, part, sems = refs[-4:]
    rows, base = own.shape[1], out.shape[0] // 2
    kinds = (near, (from_down, below), (above, from_up), (from_up, from_down))

    def average(partner):
        loads = []
        for half in range(2):
            loads.append(pltpu.make_async_copy(new[half], own.at[half], sems.at[0, half]))
            loads.append(pltpu.make_async_copy(partner[half], part.at[half], sems.at[1, half]))
        for load in loads:
            load.start()
        stores = []
        for half in range(2):
            loads[2 * half].wait()
            loads[2 * half + 1].wait()

            def body(number, carry, half=half):
                at = pl.ds(pl.multiple_of(number * 64, 64), 64)
                own[half, at] = (own[half, at] + part[half, at]) * 0.5
                return carry

            lax.fori_loop(0, rows // 64, body, 0)
            place = out.at[pl.ds(half * base + begin, rows)]
            stores.append(pltpu.make_async_copy(own.at[half], place, sems.at[2, half]))
            stores[half].start()
        for store in stores:
            store.wait()

    for kind, partner in enumerate(kinds):

        @pl.when(case_ref[0] == kind)
        def _(partner=partner):
            average(partner)


def averaged(kernel, case, own, own_specs, sources, begin, end, shape, out):
    rows, columns = shape
    first, blocks = begin // BLOCK, (end - begin) // BLOCK
    base = rows // (2 * BLOCK)
    block = (BLOCK, columns)

    def near_map(wanted):
        def index(half, i, case_ref):
            used = (half == wanted) & (case_ref[0] == 0)
            return (jnp.where(used, wanted * base + first + i, 0), 0)

        return index

    def part_map(number):
        def index(half, i, case_ref):
            return (jnp.where(source_of(half, case_ref[0]) == number, i, 0), 0)

        return index

    in_specs = own_specs + [pl.BlockSpec(block, near_map(wanted)) for wanted in range(2)]
    in_specs += [pl.BlockSpec(block, part_map(number)) for number in range(1, 5)]
    operands = [case.reshape(1), *own, *sources]
    aliases = {}
    if out is not None:
        in_specs.append(pl.BlockSpec(memory_space=pl.ANY))
        aliases = {len(operands): 0}
        operands.append(out)
    size = 2 * blocks * BLOCK * columns
    return pl.pallas_call(
        kernel,
        grid_spec=pltpu.PrefetchScalarGridSpec(
            num_scalar_prefetch=1,
            grid=(2, blocks),
            in_specs=in_specs,
            out_specs=pl.BlockSpec(block, lambda half, i, case_ref: (half * base + first + i, 0)),
        ),
        out_shape=jax.ShapeDtypeStruct(shape, jnp.bfloat16),
        input_output_aliases=aliases,
        cost_estimate=pl.CostEstimate(flops=4 * size, bytes_accessed=6 * size, transcendentals=0),
        compiler_params=pltpu.CompilerParams(vmem_limit_bytes=40 << 20),
    )(*operands)


def averaged_weights(case, scales, weights, slopes, grads, sources, begin, end, out):
    rows, columns = weights.shape
    depth, base, short = slopes[0].shape[0], rows // (2 * BLOCK), slopes[1].shape[1] // (2 * BLOCK)
    first = begin // BLOCK
    fixed = pl.BlockSpec((depth, columns), lambda half, i, case_ref: (0, 0))
    own_specs = [
        pl.BlockSpec(memory_space=pltpu.SMEM),
        pl.BlockSpec((BLOCK, columns), lambda half, i, case_ref: (half * base + first + i, 0)),
        pl.BlockSpec((depth, BLOCK), lambda half, i, case_ref: (0, half * base + first + i)),
        pl.BlockSpec((depth, BLOCK), lambda half, i, case_ref: (0, half * short + first + i)),
        fixed,
        fixed,
    ]
    own = (scales, weights, *slopes, *grads)
    return averaged(average_kernel, case, own, own_specs, sources, begin, end, weights.shape, out)


def averaged_updates(case, own, sources, begin, end, shape, out):
    block = (2, end - begin, shape[1])
    anywhere = pl.BlockSpec(memory_space=pl.ANY)
    size = (end - begin) * shape[1]
    return pl.pallas_call(
        partial(plain_kernel, begin),
        in_specs=[pl.BlockSpec(memory_space=pltpu.SMEM)] + [anywhere] * 9,
        out_specs=anywhere,
        out_shape=jax.ShapeDtypeStruct(shape, jnp.bfloat16),
        input_output_aliases={9: 0},
        scratch_shapes=[
            pltpu.VMEM(block, jnp.bfloat16),
            pltpu.VMEM(block, jnp.bfloat16),
            pltpu.SemaphoreType.DMA((3, 2)),
        ],
        cost_estimate=pl.CostEstimate(flops=4 * size, bytes_accessed=12 * size, transcendentals=0),
        compiler_params=pltpu.CompilerParams(vmem_limit_bytes=24 << 20),
    )(case.reshape(1), *own, *sources, out)


def squares_kernel(slope, grad, key_grad, out, total):
    step = pl.program_id(0)

    @pl.when(step == 0)
    def _():
        total[...] = jnp.zeros_like(total)

    rows = slope[...].T
    columns = grad.shape[1]

    def added(grads):
        gradient = dot(rows, grads, ROWS_COLS)
        return jnp.sum((gradient * gradient).reshape(-1, 8, gradient.shape[1]), axis=0)

    def strip(number, carry):
        cols = pl.ds(pl.multiple_of(number * STRIP, STRIP), STRIP)
        total[...] += added(grad[:, cols])
        return carry

    lax.fori_loop(0, columns // STRIP, strip, 0)
    total[:, :HEAD] += added(key_grad[...]) * 0.5

    @pl.when(step == pl.num_programs(0) - 1)
    def _():
        out[...] = jnp.sum(total[...], keepdims=True)


def gradient_squares(slope, grad, key_grad):
    depth, rows = slope.shape
    in_scale = rows ** (-0.5)
    size = rows * (grad.shape[1] + HEAD) * depth
    block = rows // 3
    squares = pl.pallas_call(
        squares_kernel,
        grid=(rows // block,),
        in_specs=[
            pl.BlockSpec((depth, block), lambda i: (0, i)),
            pl.BlockSpec(grad.shape, lambda i: (0, 0)),
            pl.BlockSpec(key_grad.shape, lambda i: (0, 0)),
        ],
        out_specs=pl.BlockSpec((1, 1), lambda i: (0, 0)),
        out_shape=jax.ShapeDtypeStruct((1, 1), jnp.float32),
        scratch_shapes=[pltpu.VMEM((8, STRIP), jnp.float32)],
        cost_estimate=pl.CostEstimate(
            flops=2 * size, bytes_accessed=2 * slope.size + 2 * grad.size, transcendentals=0
        ),
        compiler_params=pltpu.CompilerParams(vmem_limit_bytes=16 << 20),
    )(slope, grad, key_grad)
    return squares[0, 0] * (in_scale * in_scale)


def source_of(half, case):
    up = jnp.where(case == 1, 4, jnp.where(case == 2, 1, 3))
    down = jnp.where(case == 1, 2, jnp.where(case == 2, 3, 4))
    return jnp.where(case == 0, 0, jnp.where(half == 0, up, down))


def settled_kernel(a_ref, b_ref, c_ref, d_ref):
    c_ref[...] = a_ref[...]
    d_ref[...] = b_ref[...]


def settled(a, b):
    block = pl.BlockSpec((64, a.shape[1]), lambda i: (i, 0))
    return pl.pallas_call(
        settled_kernel,
        grid=(a.shape[0] // 64,),
        in_specs=[block, block],
        out_specs=[block, block],
        out_shape=[jax.ShapeDtypeStruct(x.shape, x.dtype) for x in (a, b)],
        cost_estimate=pl.CostEstimate(flops=0, bytes_accessed=8 * a.size, transcendentals=0),
        compiler_params=pltpu.CompilerParams(vmem_limit_bytes=8 << 20),
    )(a, b)


def section(fwd_in, bwd_in, bwd_grad, seg_fwd, seg_bwd, w_query, w_key, gain, gossip_exp):
    query_weight = w_query[0, 0]
    key_weight = w_key[0, 0]
    gain_local = gain[0, 0]
    fwd_rows = fwd_in[0, 0]
    bwd_rows = bwd_in[0, 0]
    grad_rows = bwd_grad[0, 0]
    count, local_width = fwd_rows.shape
    pipe_count = lax.axis_size("pipe")
    tp_index = lax.axis_index("tp")
    low = tp_index == 0
    offset = tp_index * local_width
    gossip = Gossip(gossip_exp[0])

    width = query_weight.shape[0]
    in_scale = width ** (-0.5)
    half, early_rows = width // 2, width // 4
    cuts = ((early_rows, half - EDGE), (half - EDGE, half))
    pieces, sent = ((0, BLOCK), (BLOCK, early_rows)), []
    for begin, end in pieces:
        parts = cut_out(query_weight, begin, end)
        sent.append(gossip.first(*parts))
    near = flipped(query_weight, "rep", 0)

    beside = jnp.broadcast_to(gain_local[None], (16, local_width))
    other = flipped(jnp.concatenate([bwd_rows, beside], axis=0), "tp", 0)
    bwd_full = in_order(bwd_rows, other[:count], low, 1)
    gain_full = in_order(gain_local, other[count], low, 0)

    _, scaled_b, inv_b, normed_b = normalize(bwd_full, gain_full)
    own_values_b = lax.dynamic_slice_in_dim(normed_b, offset, local_width, 1)
    key_rows = lax.dynamic_slice_in_dim(key_weight, offset, local_width, 0)
    early = gossip.small(own_values_b[:, :early_rows])
    early_other = flipped(early, "tp", 0)
    normed_partner = in_order(early, early_other, low, 1)

    queries = projected(normed_b, query_weight)
    keys = projected(normed_b, key_weight)
    query_grad, value_grad, key_part = per_head(
        back_kernel,
        seg_bwd[0, 0],
        queries,
        keys,
        (own_values_b, grad_rows),
        (
            ((count, local_width), jnp.bfloat16),
            ((count, local_width), jnp.float32),
            ((count, HEAD), jnp.bfloat16),
        ),
        5,
    )

    query_grad_partner = gossip.small(query_grad)
    key_other = flipped(key_part, "tp", 0)
    key_grad = (key_part.astype(jnp.float32) + key_other.astype(jnp.float32)).astype(jnp.bfloat16)

    contract_last = (((1,), (1,)), ((), ()))
    partial_grad = (
        lax.dot_general(query_grad, query_weight, contract_last, preferred_element_type=jnp.float32)
        * in_scale
    )
    own_part = (lax.dynamic_slice_in_dim(partial_grad, offset, local_width, 1) + value_grad).astype(
        jnp.bfloat16
    )
    other_part = lax.dynamic_slice_in_dim(
        partial_grad, local_width - offset, local_width, 1
    ).astype(jnp.bfloat16)
    from_other = flipped(other_part, "tp", 0)
    full_grad = (
        own_part.astype(jnp.float32)
        + from_other.astype(jnp.float32)
        + lax.dot_general(key_grad, key_rows, contract_last, preferred_element_type=jnp.float32)
        * in_scale
    )
    own_scaled = lax.dynamic_slice_in_dim(scaled_b, offset, local_width, 1)
    weighted = full_grad * gain_local.astype(jnp.float32)
    sums = jnp.stack([jnp.sum(weighted, axis=-1), jnp.sum(weighted * own_scaled, axis=-1)])
    means = (sums + flipped(sums, "tp", 0)) / width
    input_grad = inv_b * (weighted - means[0][:, None] - own_scaled * means[1][:, None])
    grad_gain = jnp.sum(full_grad * own_scaled, axis=0)
    back_rows = (grad_rows.astype(jnp.float32) + input_grad).astype(jnp.bfloat16)
    prev_rows = from_behind(back_rows, "pipe", -1)

    contract_first = (((0,), (0,)), ((), ()))

    def weight_grad(rows, grad):
        return (
            lax.dot_general(rows, grad, contract_first, preferred_element_type=jnp.float32)
            * in_scale
        )

    query_squares = gradient_squares(normed_b, query_grad, key_grad)
    grad_key = weight_grad(own_values_b, key_grad)
    local_squares = query_squares + jnp.sum(grad_gain * grad_gain)
    fwd_other = flipped(fwd_rows, "tp", 0)
    fwd_other, _ = lax.optimization_barrier((fwd_other, local_squares))
    fwd_full = in_order(fwd_rows, fwd_other, low, 1)
    _, _, _, normed = normalize(fwd_full, gain_full)
    own_values = lax.dynamic_slice_in_dim(normed, offset, local_width, 1)
    queries_f = projected(normed, query_weight)
    keys_f = projected(normed, key_weight)
    (section_out,) = per_head(
        onward_kernel,
        seg_fwd[0, 0],
        queries_f,
        keys_f,
        (own_values, fwd_rows),
        (((count, local_width), jnp.bfloat16),),
        2,
    )
    next_rows = from_behind(section_out, "pipe", 1)

    total_squares = of_everyone(local_squares, ("pipe", "tp"))
    total = pipe_count * (width * width + width * HEAD + width)
    inverse = lax.rsqrt(total_squares / total + STEP_EPS)

    def step_of(gradient, scale):
        return (LEARN_RATE * gradient * scale).astype(jnp.bfloat16)

    gain_new = updated(gain_local, step_of(grad_gain, inverse))
    both = gossip.tiny(
        jnp.concatenate([gain_new.astype(jnp.float32), jnp.broadcast_to(inverse, (HEAD,))])
    )
    gain_partner = both[:local_width].astype(jnp.bfloat16)
    inverse_partner = both[local_width]
    gain_out = halves(gain_new, gain_partner)

    key_new = updated(key_rows, step_of(grad_key, inverse))
    key_half = halves(key_new, gossip.small(key_new))
    key_out = in_order(key_half, flipped(key_half, "tp", 0), low, 0)

    news = []
    for begin, end in cuts:
        new = renewed(inverse.reshape(1), query_weight, normed_b, query_grad, begin, end)
        state = gossip.first(*new)
        new_near = [flipped(part, "rep", 0) for part in new]
        later = gossip.second(state)
        news.append((new, (*new_near, *later)))

    passed = []
    for state in sent:
        passed.append((near, near, *gossip.second(state)))
    next_rows, prev_rows = settled(next_rows, prev_rows)
    query_out = None
    for number, (begin, end) in enumerate(pieces):
        query_out = averaged_weights(
            gossip.case,
            jnp.stack([inverse, inverse_partner]),
            query_weight,
            (normed_b, normed_partner),
            (query_grad, query_grad_partner),
            passed[number],
            begin,
            end,
            query_out,
        )
    for number, (begin, end) in enumerate(cuts):
        query_out = averaged_updates(
            gossip.case, *news[number], begin, end, query_weight.shape, query_out
        )
    return (
        next_rows[None, None],
        prev_rows[None, None],
        query_out[None, None],
        key_out[None, None],
        gain_out[None, None],
    )


def solution(mesh):
    return jax.shard_map(
        section,
        mesh=mesh,
        in_specs=(
            P("rep", "pipe", None, "tp"),
            P("rep", "pipe", None, "tp"),
            P("rep", "pipe", None, "tp"),
            P("rep", "pipe", None),
            P("rep", "pipe", None),
            P("rep", "pipe", None, "tp"),
            P("rep", "pipe", None, None),
            P("rep", "pipe", "tp"),
            P("pipe"),
        ),
        out_specs=(
            P("rep", "pipe", None, "tp"),
            P("rep", "pipe", None, "tp"),
            P("rep", "pipe", None, "tp"),
            P("rep", "pipe", None, None),
            P("rep", "pipe", "tp"),
        ),
        check_vma=False,
    )
```
